256 devices in a mesh: dp: 8 (over z_lo, y), expert: 32 (over x, z_hi, core).
Axes of the slice: x: 4, y: 4, z: 8 (z_hi: 4, z_lo: 2; z = z_hi * 2 + z_lo), core: 2. Of those that a mesh axis runs over, the one named last changes fastest.
Arguments:
- x_tokens: bfloat16 [32768, 2048], P(('dp', 'expert')), may hold values from -6 to 6
- dy_tokens: bfloat16 [32768, 2048], P(('dp', 'expert')), may hold values from -24 to 24
- probs: bfloat16 [32768, 8], P(('dp', 'expert')), may hold values from 0.049804688 to 0.5
- ids: int32 [32768, 8], P(('dp', 'expert')), may hold values from 0 to 127, all different within a row
- w_gate: bfloat16 [32, 2048, 768], P('expert'), may hold values from -0.125 to 0.125
- w_up: bfloat16 [32, 2048, 768], P('expert'), may hold values from -0.125 to 0.125
- w_down: bfloat16 [32, 2048, 768], P('expert'), may hold values from -0.21875 to 0.21875
Outputs:
- x_grad: bfloat16 [32768, 2048], P(('dp', 'expert'))
- gate_grad: float32 [32, 2048, 768], P('expert', 'dp')
- up_grad: float32 [32, 2048, 768], P('expert', 'dp')
- down_grad: float32 [32, 2048, 768], P('expert', 'dp')
The draws below stay inside these ranges and needn't reach their ends.
Inputs may be any that keep to these rules, and one draw needn't show every extreme that they name: `ids`: each row names 8 different experts.
All inputs are finite; a program needn't handle non-finite values.
Results may differ from the reference program's by a relative error of at most 0.0063.
Values may be sent and summed in bfloat16 or wider, within the bound.
A program may use at most 128 MiB of HBM per device.

```python
import math
import jax
import jax.numpy as jnp
from jax import lax

D = 2048
HW = 768
ALL_EXPERTS = 128
TOP = 8
TOK_DEV = 128
CAP = 10
EXPERTS_WIN = 32
TOKENS = 32768


def steps_of(key, shape, cuts, low, largest):
    def one(dim, blocks):
        heights = jax.random.uniform(jax.random.fold_in(jax.random.fold_in(key, 6), dim), (blocks,), jnp.float32, low / len(cuts), largest / len(cuts))
        return jnp.repeat(jnp.exp(heights), shape[dim] // blocks).reshape((-1,) + (1,) * (len(shape) - dim - 1))

    gain = one(*cuts[0])
    for cut in cuts[1:]:
        gain = gain * one(*cut)
    return gain


def picks_of(own_key, rows, count, top, lift):
    order = jax.random.permutation(jax.random.fold_in(own_key, 1), count)
    pull = order
    for power in range(3):
        pull = pull * pull // count
    pull = pull * lift // count
    lots = jax.random.randint(jax.random.fold_in(own_key, 2), (rows, count), 0, 4096) + pull
    sure = jax.random.permutation(jax.random.fold_in(own_key, 3), rows)[jnp.arange(count) % rows]
    lots = jnp.where(jnp.arange(rows)[:, None] == sure[None, :], 1 << 14, lots)
    priority = lots * count + jnp.arange(count)
    return lax.top_k(priority.astype(jnp.int32), top)[1].astype(jnp.int32)


def noise(stream_key, shape, width, reach, pieces=(), kind=jnp.bfloat16):
    result = jax.random.normal(stream_key, shape, jnp.float32) * width
    if len(pieces) > 0:
        result = steps_of(stream_key, shape, pieces, -0.22, 0.18) * result
    return jnp.clip(result, min=-reach, max=reach).astype(kind)


def setup_inputs(seed: int = 0) -> dict:
    arg_keys = jax.random.split(jax.random.key(seed), 8)
    return {
        "x_tokens": noise(arg_keys[0], (TOKENS, D), 1.0, 6.0, ((0, 256),)),
        "dy_tokens": noise(arg_keys[1], (TOKENS, D), 4.0, 24.0, ((0, 256),)),
        "probs": jnp.clip(jnp.exp(math.log(0.5) - 2.306499 * jax.random.uniform(arg_keys[2], (TOKENS, TOP), jnp.float32) ** steps_of(arg_keys[2], (TOKENS, TOP), ((0, 256),), -0.2, 0.2)), 0.049804688, 0.5).astype(jnp.bfloat16),
        "ids": picks_of(arg_keys[3], TOKENS, ALL_EXPERTS, TOP, 1024),
        "w_gate": noise(arg_keys[4], (EXPERTS_WIN, D, HW), D ** -0.5, 0.125, ((0, 32),)),
        "w_up": noise(arg_keys[5], (EXPERTS_WIN, D, HW), D ** -0.5, 0.125, ((0, 32),)),
        "w_down": noise(arg_keys[6], (EXPERTS_WIN, D, HW), HW ** -0.5, 0.21875, ((0, 32),)),
    }


def expert_pass(expert_rows, out_grads, gate_scale, gate_mat, up_mat, down_mat):
    gate_pre = jnp.dot(expert_rows, gate_mat, preferred_element_type=jnp.float32)
    up_pre = jnp.dot(expert_rows, up_mat, preferred_element_type=jnp.float32)
    gate_sig = jax.nn.sigmoid(gate_pre)
    gate_act = gate_pre * gate_sig
    hidden = (gate_act * up_pre).astype(jnp.bfloat16)
    scaled = (gate_scale[:, None].astype(jnp.float32) * out_grads.astype(jnp.float32)).astype(jnp.bfloat16)
    hidden_grad = jnp.dot(scaled, down_mat, preferred_element_type=jnp.float32)
    up_delta = (hidden_grad * gate_act).astype(jnp.bfloat16)
    gate_delta = (hidden_grad * up_pre * gate_sig * (1.0 + gate_pre * (1.0 - gate_sig))).astype(jnp.bfloat16)
    dims = (((1,), (1,)), ((), ()))
    slot_back = lax.dot_general(gate_delta, gate_mat, dims, preferred_element_type=jnp.float32)
    slot_back = slot_back + lax.dot_general(up_delta, up_mat, dims, preferred_element_type=jnp.float32)
    return hidden, scaled, gate_delta, up_delta, slot_back.astype(jnp.bfloat16)


def reference(x_tokens, dy_tokens, probs, ids, w_gate, w_up, w_down):
    blocks = TOKENS // TOK_DEV
    per_block = TOK_DEV * TOP
    slot_count = EXPERTS_WIN * CAP
    flat_ids = ids.reshape(blocks, per_block)
    experts = jnp.arange(EXPERTS_WIN, dtype=jnp.int32)
    onehot = (flat_ids[:, :, None] == experts[None, None, :]).astype(jnp.int32)
    slot_rank = jnp.sum((jnp.cumsum(onehot, axis=1) - onehot) * onehot, axis=2).astype(jnp.int32)
    kept_mask = (flat_ids < EXPERTS_WIN) & (slot_rank < CAP)
    target = jnp.where(kept_mask, flat_ids * CAP + slot_rank, slot_count).astype(jnp.int32)
    block_ids = jnp.arange(blocks, dtype=jnp.int32)[:, None]
    positions = jnp.broadcast_to(jnp.arange(per_block, dtype=jnp.int32)[None, :], (blocks, per_block))
    slot_table = jnp.full((blocks, slot_count + 1), -1, jnp.int32).at[block_ids, target].set(positions)
    slot_table = slot_table[:, :slot_count]
    valid_slot = slot_table >= 0
    token_index = jnp.where(valid_slot, block_ids * TOK_DEV + slot_table // TOP, TOKENS).astype(jnp.int32)
    assign_index = jnp.where(valid_slot, block_ids * per_block + slot_table, 0).astype(jnp.int32)
    prob_flat = probs.reshape(-1)

    def one_expert(running, inputs):
        expert_id, gate_mat, up_mat, down_mat = inputs
        token_pos = lax.dynamic_slice_in_dim(token_index, expert_id * CAP, CAP, 1).reshape(-1)
        assign_pos = lax.dynamic_slice_in_dim(assign_index, expert_id * CAP, CAP, 1).reshape(-1)
        live_slot = token_pos < TOKENS
        safe_pos = jnp.where(live_slot, token_pos, 0).astype(jnp.int32)
        zero_value = jnp.zeros((), jnp.bfloat16)
        expert_rows = jnp.where(live_slot[:, None], x_tokens[safe_pos], zero_value)
        out_grads = jnp.where(live_slot[:, None], dy_tokens[safe_pos], zero_value)
        gate_scale = jnp.where(live_slot, prob_flat[assign_pos], zero_value)
        hidden, scaled, gate_delta, up_delta, slot_back = expert_pass(expert_rows, out_grads, gate_scale, gate_mat, up_mat, down_mat)
        running = running.at[token_pos].add(slot_back.astype(jnp.float32), mode="drop")
        gate_part = jnp.dot(expert_rows.T, gate_delta, preferred_element_type=jnp.float32)
        up_part = jnp.dot(expert_rows.T, up_delta, preferred_element_type=jnp.float32)
        down_part = jnp.dot(scaled.T, hidden, preferred_element_type=jnp.float32)
        return running, (gate_part, up_part, down_part)

    running, grads_all = lax.scan(one_expert, jnp.zeros((TOKENS, D), jnp.float32), (experts, w_gate, w_up, w_down))
    return running.astype(jnp.bfloat16), grads_all[0], grads_all[1], grads_all[2]
```

```python
import functools

import jax
import jax.numpy as jnp
import numpy as np
from jax import lax
from jax.experimental import pallas as pl
from jax.experimental.pallas import tpu as pltpu
from jax.sharding import PartitionSpec as P

MESH = pl.DeviceIdType.MESH
F32, BF16 = jnp.float32, jnp.bfloat16
CAP = 10
TOK = 128
D = 2048
HW = 768
NX = 4
ZC = 8
NY = 4
CB = 8
CW = D // CB
ROWS = ZC * CAP
CHUNK = CB * CAP
GROUP = ZC * CHUNK
SLOTS = NX * ROWS
HALF = 2 * ROWS


def dot(a, b, ca=1, cb=0):
    return lax.dot_general(a, b, (((ca,), (cb,)), ((), ())), preferred_element_type=F32)


def kernel(
    ids_ref, p_ref, tgt_ref, inv_ref, x_ref, dy_ref, wg_hbm, wu_hbm, wd_hbm,
    xg_ref, gg_ref, ug_ref, dg_ref,
    wgu, wd, pick, pickp, toa, tos,
    s_x, r_x, s_s, r_s, s_b, r_b, a_x, a_s, a_b,
    act, gfac, hid, gu, xs, ss, dh, dgu, z_s, z_r,
    wsem, lsem, sx_sem, rx_sem, sd_sem, rd_sem, sb_sem, rb_sem,
    yx_s, yx_r, ys_s, ys_r, yh_s, yh_r, yg_s, yg_r, zz_s, zz_r,
):
    dpi = lax.axis_index("dp")
    me = lax.axis_index("expert")
    zl, y = dpi // NY, lax.rem(dpi, NY)
    xi, zc = me // ZC, lax.rem(me, ZC)

    loads = [
        pltpu.make_async_copy(wg_hbm.at[0], wgu.at[:, pl.ds(0, HW)], wsem.at[0]),
        pltpu.make_async_copy(wu_hbm.at[0], wgu.at[:, pl.ds(HW, HW)], wsem.at[1]),
        pltpu.make_async_copy(wd_hbm.at[0], wd, wsem.at[2]),
    ]
    for load in loads:
        load.start()

    barrier = pltpu.get_barrier_semaphore()
    for k in range(1, NX * ZC):
        pl.semaphore_signal(
            barrier, inc=1, device_id=(dpi, lax.rem(me + k, NX * ZC)), device_id_type=MESH
        )
    for k in range(1, NY):
        pl.semaphore_signal(
            barrier, inc=1, device_id=(zl * NY + lax.rem(y + k, NY), me), device_id_type=MESH
        )
    partner = (1 - zl) * NY + y
    pl.semaphore_signal(barrier, inc=1, device_id=(partner, me), device_id_type=MESH)

    row = lax.broadcasted_iota(jnp.int32, (NX * ZC, TOK), 0)
    expert = row + ZC * xi
    expert = jnp.where(expert >= NX * ZC, expert - NX * ZC, expert)
    member = jnp.zeros((NX * ZC, TOK), F32)
    weight = jnp.zeros((NX * ZC, TOK), F32)
    probs = p_ref[...].astype(F32)
    for k in range(8):
        same = ids_ref[k : k + 1, :] == expert
        member = jnp.where(same, 1.0, member)
        weight = jnp.where(same, probs[k : k + 1, :], weight)
    before = lax.broadcasted_iota(jnp.int32, (TOK, TOK), 0) < lax.broadcasted_iota(
        jnp.int32, (TOK, TOK), 1
    )
    rank = dot(member.astype(BF16), jnp.where(before, 1.0, 0.0).astype(BF16))
    rank = jnp.where(member > 0.5, rank, -1.0).astype(BF16)
    slot = lax.broadcasted_iota(jnp.int32, (SLOTS, NX * ZC), 0)
    first = CAP * lax.broadcasted_iota(jnp.int32, (SLOTS, NX * ZC), 1)
    spread = jnp.where((slot >= first) & (slot < first + CAP), 1.0, 0.0).astype(BF16)
    of_rank = dot(spread, rank)
    of_weight = dot(spread, weight.astype(BF16))
    of_row = dot(spread, row.astype(F32).astype(BF16))
    place = lax.broadcasted_iota(jnp.int32, (SLOTS, TOK), 0).astype(F32) - CAP * of_row
    hit = of_rank == place
    pick[...] = jnp.where(hit, 1.0, 0.0).astype(BF16)
    pickp[...] = jnp.where(hit, of_weight, 0.0).astype(BF16)
    down = lax.broadcasted_iota(jnp.int32, (GROUP, GROUP), 0)
    tos[...] = jnp.where(down == tgt_ref[...], 1.0, 0.0).astype(BF16)
    toa[...] = jnp.where(down == inv_ref[...], 1.0, 0.0).astype(BF16)

    def exchange(src, dst, send, recv, j, i, sign):
        zt = lax.rem(zc + i, ZC)
        xt = lax.rem(xi + sign * j + NX, NX)
        from_rows = pl.ds(pl.multiple_of((j * ZC + zt) * CHUNK, 16), CHUNK)
        to_rows = pl.ds(pl.multiple_of((j * ZC + zc) * CHUNK, 16), CHUNK)
        if i == 0 and j == 0:
            return pltpu.make_async_copy(src.at[from_rows], dst.at[to_rows], recv.at[0])
        return pltpu.make_async_remote_copy(
            src_ref=src.at[from_rows],
            dst_ref=dst.at[to_rows],
            send_sem=send.at[j * ZC + i],
            recv_sem=recv.at[j * ZC + i],
            device_id=(dpi, xt * ZC + zt),
            device_id_type=MESH,
        )

    sent = []

    def start_group(src, dst, send, recv, j, sign):
        for i in range(ZC):
            copy = exchange(src, dst, send, recv, j, i, sign)
            copy.start()
            if i or j:
                sent.append(copy)

    def wait_group(src, dst, send, recv, j, sign):
        for i in range(ZC):
            copy = exchange(src, dst, send, recv, j, i, sign)
            if i or j:
                copy.wait_recv()
            else:
                copy.wait()

    def pack(blocks):
        return dot(tos[...], jnp.concatenate(blocks, axis=0)).astype(BF16)

    def unpack(src, dst, j):
        rows = dot(toa[...], src[j * GROUP : (j + 1) * GROUP, :]).astype(BF16)
        for c in range(CB):
            dst[c, j * ROWS : (j + 1) * ROWS, :] = rows[c * ROWS : (c + 1) * ROWS, :]

    def gather(sel, tokens, dst, j):
        rows = dot(sel[j * ROWS : (j + 1) * ROWS, :], tokens[...]).astype(BF16)
        dst[j * GROUP : (j + 1) * GROUP, :] = pack(
            [rows[:, c * CW : (c + 1) * CW] for c in range(CB)]
        )

    for j in range(NX):
        gather(pick, x_ref, s_x, j)
        if j == 0:
            pl.semaphore_wait(barrier, NX * ZC - 1 + NY)
        start_group(s_x, r_x, sx_sem, rx_sem, j, 1)
    for j in range(NX):
        gather(pickp, dy_ref, s_s, j)
        start_group(s_s, r_s, sd_sem, rd_sem, j, 1)

    def to_y(src, dst, send, recv, k):
        return pltpu.make_async_remote_copy(
            src_ref=src,
            dst_ref=dst,
            send_sem=send,
            recv_sem=recv,
            device_id=(zl * NY + lax.rem(y + k, NY), me),
            device_id_type=MESH,
        )

    def slice_copy(src, dst, send, recv, k, b, h):
        part = pl.ds(h * HALF, HALF)
        n = (k * 2 + b) * 2 + h
        yt = lax.rem(y + k, NY)
        return to_y(
            src.at[b * NY + yt, part], dst.at[k, b, part], send.at[n], recv.at[n], k
        )

    def start_slices(src, dst, send, recv, h):
        for k in range(1, NY):
            for b in range(2):
                copy = slice_copy(src, dst, send, recv, k, b, h)
                copy.start()
                sent.append(copy)

    def wait_slices(src, dst, send, recv):
        for h in range(2):
            for k in range(1, NY):
                for b in range(2):
                    slice_copy(src, dst, send, recv, k, b, h).wait_recv()

    for h in range(2):
        for j in (2 * h, 2 * h + 1):
            wait_group(s_x, r_x, sx_sem, rx_sem, j, 1)
            unpack(r_x, a_x, j)
        start_slices(a_x, xs, yx_s, yx_r, h)

    for load in loads:
        load.wait()
    for h in range(2):
        part = slice(h * HALF, (h + 1) * HALF)
        rows = jnp.concatenate([a_x[c, part, :] for c in range(CB)], axis=1)
        for n in range(HW // CW):
            cols = slice(n * CW, (n + 1) * CW)
            gate_pre = dot(rows, wgu[:, n * CW : (n + 1) * CW])
            up_pre = dot(rows, wgu[:, HW + n * CW : HW + (n + 1) * CW])
            sig = 1.0 / (1.0 + jnp.exp(-gate_pre))
            gate_act = gate_pre * sig
            act[part, cols] = gate_act
            gfac[part, cols] = up_pre * sig * (1.0 + gate_pre * (1.0 - sig))
            hid[part, cols] = (gate_act * up_pre).astype(BF16)

    def hid_copy(k):
        return to_y(hid, dh.at[k], yh_s.at[k], yh_r.at[k], k)

    def gu_copy(k, h):
        part = pl.ds(h * HALF, HALF)
        return to_y(gu.at[part], dgu.at[k, part], yg_s.at[2 * k + h], yg_r.at[2 * k + h], k)

    for k in range(1, NY):
        hid_copy(k).start()
        sent.append(hid_copy(k))

    for h in range(2):
        part = slice(h * HALF, (h + 1) * HALF)
        for j in (2 * h, 2 * h + 1):
            wait_group(s_s, r_s, sd_sem, rd_sem, j, 1)
            unpack(r_s, a_s, j)
        start_slices(a_s, ss, ys_s, ys_r, h)
        rows = jnp.concatenate([a_s[c, part, :] for c in range(CB)], axis=1)
        for n in range(HW // CW):
            cols = slice(n * CW, (n + 1) * CW)
            hidden_grad = dot(rows, wd[:, n * CW : (n + 1) * CW])
            gu[part, cols] = (hidden_grad * gfac[part, cols]).astype(BF16)
            gu[part, HW + n * CW : HW + (n + 1) * CW] = (hidden_grad * act[part, cols]).astype(BF16)
        for k in range(1, NY):
            gu_copy(k, h).start()
            sent.append(gu_copy(k, h))
        deltas = gu[part, :]
        back = [
            dot(deltas, wgu[c * CW : (c + 1) * CW, :], 1, 1).astype(BF16) for c in range(CB)
        ]
        for g in range(2):
            j = 2 * h + g
            s_b[j * GROUP : (j + 1) * GROUP, :] = pack(
                [block[g * ROWS : (g + 1) * ROWS, :] for block in back]
            )
            start_group(s_b, r_b, sb_sem, rb_sem, j, -1)

    def z_copy(n):
        return pltpu.make_async_remote_copy(
            src_ref=z_s.at[n],
            dst_ref=z_r.at[n],
            send_sem=zz_s.at[n],
            recv_sem=zz_r.at[n],
            device_id=(partner, me),
            device_id_type=MESH,
        )

    def sums(slices, own, b, right):
        total = dot(own[b * NY + y], right(0), 0, 0)
        for k in range(1, NY):
            total = total + dot(slices[k, b], right(k), 0, 0)
        return total

    outs = (gg_ref, ug_ref, dg_ref)
    wait_slices(a_s, ss, ys_s, ys_r)
    for k in range(1, NY):
        hid_copy(k).wait_recv()

    def hid_of(k):
        return hid[...] if k == 0 else dh[k]

    z_s[2] = sums(ss, a_s, 1 - zl, hid_of).astype(BF16)
    z_copy(2).start()
    sent.append(z_copy(2))
    dg_ref[...] = sums(ss, a_s, zl, hid_of)

    wait_slices(a_x, xs, yx_s, yx_r)
    for h in range(2):
        for k in range(1, NY):
            gu_copy(k, h).wait_recv()
    for n in range(2):

        def gu_of(k):
            cols = slice(n * HW, (n + 1) * HW)
            return gu[:, cols] if k == 0 else dgu[k, :, cols]

        z_s[n] = sums(xs, a_x, 1 - zl, gu_of).astype(BF16)
        z_copy(n).start()
        sent.append(z_copy(n))
    for n in range(2):

        def gu_of(k):
            cols = slice(n * HW, (n + 1) * HW)
            return gu[:, cols] if k == 0 else dgu[k, :, cols]

        outs[n][...] = sums(xs, a_x, zl, gu_of)

    for j in range(NX):
        wait_group(s_b, r_b, sb_sem, rb_sem, j, -1)
        unpack(r_b, a_b, j)
    for c in range(CB):
        xg_ref[:, c * CW : (c + 1) * CW] = dot(pick[...], a_b[c], 0, 0).astype(BF16)
    for n in (2, 0, 1):
        z_copy(n).wait_recv()
        outs[n][...] += z_r[n].astype(F32)
    for copy in sent:
        copy.wait_send()


def on_device(x_tokens, dy_tokens, probs, ids, w_gate, w_up, w_down):
    r = np.arange(GROUP)
    c, rest = r // ROWS, r % ROWS
    tgt = (rest // CAP) * CHUNK + c * CAP + rest % CAP
    inv = np.argsort(tgt)
    vmem = pl.BlockSpec(memory_space=pltpu.VMEM)
    anywhere = pl.BlockSpec(memory_space=pl.ANY)
    dma = pltpu.SemaphoreType.DMA
    grad = jax.ShapeDtypeStruct((D // 8, HW), F32)
    chunks = pltpu.VMEM((NX * GROUP, CW), BF16)
    slots = pltpu.VMEM((CB, SLOTS, CW), BF16)
    x_grad, gate_grad, up_grad, down_grad = pl.pallas_call(
        kernel,
        out_shape=(jax.ShapeDtypeStruct((TOK, D), BF16), grad, grad, grad),
        in_specs=[vmem] * 6 + [anywhere] * 3,
        out_specs=[vmem] * 4,
        scratch_shapes=[
            pltpu.VMEM((D, 2 * HW), BF16),
            pltpu.VMEM((D, HW), BF16),
            pltpu.VMEM((SLOTS, TOK), BF16),
            pltpu.VMEM((SLOTS, TOK), BF16),
            pltpu.VMEM((GROUP, GROUP), BF16),
            pltpu.VMEM((GROUP, GROUP), BF16),
        ]
        + [chunks] * 6
        + [slots] * 3
        + [
            pltpu.VMEM((SLOTS, HW), F32),
            pltpu.VMEM((SLOTS, HW), F32),
            pltpu.VMEM((SLOTS, HW), BF16),
            pltpu.VMEM((SLOTS, 2 * HW), BF16),
            pltpu.VMEM((NY, 2, SLOTS, CW), BF16),
            pltpu.VMEM((NY, 2, SLOTS, CW), BF16),
            pltpu.VMEM((NY, SLOTS, HW), BF16),
            pltpu.VMEM((NY, SLOTS, 2 * HW), BF16),
            pltpu.VMEM((3, D // 8, HW), BF16),
            pltpu.VMEM((3, D // 8, HW), BF16),
            dma((3,)),
            dma((1,)),
        ]
        + [dma((NX * ZC,))] * 6
        + [dma((4 * NY,))] * 4
        + [dma((NY,))] * 2
        + [dma((2 * NY,))] * 2
        + [dma((3,))] * 2,
        compiler_params=pltpu.CompilerParams(
            collective_id=0, has_side_effects=True, vmem_limit_bytes=60 << 20
        ),
    )(
        ids.T,
        probs.T,
        jnp.asarray(tgt, jnp.int32)[None],
        jnp.asarray(inv, jnp.int32)[None],
        x_tokens,
        dy_tokens,
        w_gate,
        w_up,
        w_down,
    )
    return (x_grad, gate_grad[None], up_grad[None], down_grad[None])


def solution(mesh):
    rows = P(("dp", "expert"), None)
    held = P("expert", None, None)
    owned = P("expert", "dp", None)
    return jax.shard_map(
        on_device,
        mesh=mesh,
        in_specs=(rows, rows, rows, rows, held, held, held),
        out_specs=(rows, owned, owned, owned),
        check_vma=False,
    )
```

```python
import functools

import jax
import jax.numpy as jnp
import numpy as np
from jax import lax
from jax.experimental import pallas as pl
from jax.experimental.pallas import tpu as pltpu
from jax.sharding import PartitionSpec as P

MESH = pl.DeviceIdType.MESH
F32, BF16 = jnp.float32, jnp.bfloat16
CAP = 10
TOK = 128
D = 2048
HW = 768
NX = 4
ZC = 8
NY = 4
CB = 8
CW = D // CB
ROWS = ZC * CAP
CHUNK = CB * CAP
GROUP = ZC * CHUNK
SLOTS = NX * ROWS
HALF = 2 * ROWS


def dot(a, b, ca=1, cb=0):
    return lax.dot_general(a, b, (((ca,), (cb,)), ((), ())), preferred_element_type=F32)


def kernel(
    ids_ref, p_ref, tgt_ref, inv_ref, x_ref, dy_ref, wg_hbm, wu_hbm, wd_hbm,
    xg_hbm, own_hbm, got_hbm,
    wgu, wd, pick, pickp, toa, tos,
    s_x, r_x, s_s, r_s, s_b, r_b, a_x, a_s, a_b,
    act, gfac, hid, gu, xs, ss, dh, dgu, z_s, own, xg,
    wsem, osem, sx_sem, rx_sem, sd_sem, rd_sem, sb_sem, rb_sem,
    yx_s, yx_r, ys_s, ys_r, yh_s, yh_r, yg_s, yg_r, zz_s, zz_r,
):
    dpi = lax.axis_index("dp")
    me = lax.axis_index("expert")
    zl, y = dpi // NY, lax.rem(dpi, NY)
    xi, zc = me // ZC, lax.rem(me, ZC)

    loads = [
        pltpu.make_async_copy(wg_hbm.at[0], wgu.at[:, pl.ds(0, HW)], wsem.at[0]),
        pltpu.make_async_copy(wu_hbm.at[0], wgu.at[:, pl.ds(HW, HW)], wsem.at[1]),
        pltpu.make_async_copy(wd_hbm.at[0], wd, wsem.at[2]),
    ]
    for load in loads:
        load.start()

    barrier = pltpu.get_barrier_semaphore()
    for k in range(1, NX * ZC):
        pl.semaphore_signal(
            barrier, inc=1, device_id=(dpi, lax.rem(me + k, NX * ZC)), device_id_type=MESH
        )
    for k in range(1, NY):
        pl.semaphore_signal(
            barrier, inc=1, device_id=(zl * NY + lax.rem(y + k, NY), me), device_id_type=MESH
        )
    partner = (1 - zl) * NY + y
    pl.semaphore_signal(barrier, inc=1, device_id=(partner, me), device_id_type=MESH)

    row = lax.broadcasted_iota(jnp.int32, (NX * ZC, TOK), 0)
    expert = row + ZC * xi
    expert = jnp.where(expert >= NX * ZC, expert - NX * ZC, expert)
    member = jnp.zeros((NX * ZC, TOK), F32)
    weight = jnp.zeros((NX * ZC, TOK), F32)
    probs = p_ref[...].astype(F32)
    for k in range(8):
        same = ids_ref[k : k + 1, :] == expert
        member = jnp.where(same, 1.0, member)
        weight = jnp.where(same, probs[k : k + 1, :], weight)
    before = lax.broadcasted_iota(jnp.int32, (TOK, TOK), 0) < lax.broadcasted_iota(
        jnp.int32, (TOK, TOK), 1
    )
    rank = dot(member.astype(BF16), jnp.where(before, 1.0, 0.0).astype(BF16))
    rank = jnp.where(member > 0.5, rank, -1.0).astype(BF16)
    slot = lax.broadcasted_iota(jnp.int32, (SLOTS, NX * ZC), 0)
    first = CAP * lax.broadcasted_iota(jnp.int32, (SLOTS, NX * ZC), 1)
    spread = jnp.where((slot >= first) & (slot < first + CAP), 1.0, 0.0).astype(BF16)
    of_rank = dot(spread, rank)
    of_weight = dot(spread, weight.astype(BF16))
    of_row = dot(spread, row.astype(F32).astype(BF16))
    place = lax.broadcasted_iota(jnp.int32, (SLOTS, TOK), 0).astype(F32) - CAP * of_row
    hit = of_rank == place
    pick[...] = jnp.where(hit, 1.0, 0.0).astype(BF16)
    pickp[...] = jnp.where(hit, of_weight, 0.0).astype(BF16)
    down = lax.broadcasted_iota(jnp.int32, (GROUP, GROUP), 0)
    tos[...] = jnp.where(down == tgt_ref[...], 1.0, 0.0).astype(BF16)
    toa[...] = jnp.where(down == inv_ref[...], 1.0, 0.0).astype(BF16)

    def exchange(src, dst, send, recv, j, i, sign):
        zt = lax.rem(zc + i, ZC)
        xt = lax.rem(xi + sign * j + NX, NX)
        from_rows = pl.ds(pl.multiple_of((j * ZC + zt) * CHUNK, 16), CHUNK)
        to_rows = pl.ds(pl.multiple_of((j * ZC + zc) * CHUNK, 16), CHUNK)
        if i == 0 and j == 0:
            return pltpu.make_async_copy(src.at[from_rows], dst.at[to_rows], recv.at[0])
        return pltpu.make_async_remote_copy(
            src_ref=src.at[from_rows],
            dst_ref=dst.at[to_rows],
            send_sem=send.at[j * ZC + i],
            recv_sem=recv.at[j * ZC + i],
            device_id=(dpi, xt * ZC + zt),
            device_id_type=MESH,
        )

    sent = []

    def start_group(src, dst, send, recv, j, sign):
        for i in range(ZC):
            copy = exchange(src, dst, send, recv, j, i, sign)
            copy.start()
            if i or j:
                sent.append(copy)

    def wait_group(src, dst, send, recv, j, sign):
        for i in range(ZC):
            copy = exchange(src, dst, send, recv, j, i, sign)
            if i or j:
                copy.wait_recv()
            else:
                copy.wait()

    def pack(blocks):
        return dot(tos[...], jnp.concatenate(blocks, axis=0)).astype(BF16)

    def unpack(src, dst, j):
        rows = dot(toa[...], src[j * GROUP : (j + 1) * GROUP, :]).astype(BF16)
        for c in range(CB):
            dst[c, j * ROWS : (j + 1) * ROWS, :] = rows[c * ROWS : (c + 1) * ROWS, :]

    def gather(sel, tokens, dst, j):
        rows = dot(sel[j * ROWS : (j + 1) * ROWS, :], tokens[...]).astype(BF16)
        dst[j * GROUP : (j + 1) * GROUP, :] = pack(
            [rows[:, c * CW : (c + 1) * CW] for c in range(CB)]
        )

    for j in range(NX):
        gather(pick, x_ref, s_x, j)
        if j == 0:
            pl.semaphore_wait(barrier, NX * ZC - 1 + NY)
        start_group(s_x, r_x, sx_sem, rx_sem, j, 1)
    for j in range(NX):
        gather(pickp, dy_ref, s_s, j)
        start_group(s_s, r_s, sd_sem, rd_sem, j, 1)

    def to_y(src, dst, send, recv, k):
        return pltpu.make_async_remote_copy(
            src_ref=src,
            dst_ref=dst,
            send_sem=send,
            recv_sem=recv,
            device_id=(zl * NY + lax.rem(y + k, NY), me),
            device_id_type=MESH,
        )

    def slice_copy(src, dst, send, recv, k, b, h):
        part = pl.ds(h * HALF, HALF)
        n = (k * 2 + b) * 2 + h
        yt = lax.rem(y + k, NY)
        return to_y(
            src.at[b * NY + yt, part], dst.at[k, b, part], send.at[n], recv.at[n], k
        )

    def start_slices(src, dst, send, recv, h):
        for k in range(1, NY):
            for b in range(2):
                copy = slice_copy(src, dst, send, recv, k, b, h)
                copy.start()
                sent.append(copy)

    def wait_slices(src, dst, send, recv):
        for h in range(2):
            for k in range(1, NY):
                for b in range(2):
                    slice_copy(src, dst, send, recv, k, b, h).wait_recv()

    for h in range(2):
        for j in (2 * h, 2 * h + 1):
            wait_group(s_x, r_x, sx_sem, rx_sem, j, 1)
            unpack(r_x, a_x, j)
        start_slices(a_x, xs, yx_s, yx_r, h)

    for load in loads:
        load.wait()
    for h in range(2):
        part = slice(h * HALF, (h + 1) * HALF)
        rows = jnp.concatenate([a_x[c, part, :] for c in range(CB)], axis=1)
        for n in range(HW // CW):
            cols = slice(n * CW, (n + 1) * CW)
            gate_pre = dot(rows, wgu[:, n * CW : (n + 1) * CW])
            up_pre = dot(rows, wgu[:, HW + n * CW : HW + (n + 1) * CW])
            sig = 1.0 / (1.0 + jnp.exp(-gate_pre))
            gate_act = gate_pre * sig
            act[part, cols] = gate_act
            gfac[part, cols] = up_pre * sig * (1.0 + gate_pre * (1.0 - sig))
            hid[part, cols] = (gate_act * up_pre).astype(BF16)

    def piece_copy(src, dst, send, recv, size, k, q):
        part = pl.ds(q * size, size)
        n = k * (SLOTS // size) + q
        if k == 2:
            hop = 1 + 2 * (q % 2)
            return to_y(dst.at[hop, part], dst.at[2, part], send.at[n], recv.at[n], hop)
        return to_y(src.at[part], dst.at[k, part], send.at[n], recv.at[n], k)

    def hid_copy(k, q):
        return piece_copy(hid, dh, yh_s, yh_r, HALF, k, q)

    def gu_copy(k, q):
        return piece_copy(gu, dgu, yg_s, yg_r, ROWS, k, q)

    def begin(copy):
        copy.start()
        sent.append(copy)

    def pass_on(piece, even):
        for q, hop in ((even, 1), (even + 1, 3)):
            piece(hop, q).wait_recv()
            begin(piece(2, q))

    for q in range(2):
        begin(hid_copy(1, q))
        begin(hid_copy(3, 1 - q))

    for h in range(2):
        part = slice(h * HALF, (h + 1) * HALF)
        for j in (2 * h, 2 * h + 1):
            wait_group(s_s, r_s, sd_sem, rd_sem, j, 1)
            unpack(r_s, a_s, j)
        start_slices(a_s, ss, ys_s, ys_r, h)
        rows = jnp.concatenate([a_s[c, part, :] for c in range(CB)], axis=1)
        for n in range(HW // CW):
            cols = slice(n * CW, (n + 1) * CW)
            hidden_grad = dot(rows, wd[:, n * CW : (n + 1) * CW])
            gu[part, cols] = (hidden_grad * gfac[part, cols]).astype(BF16)
            gu[part, HW + n * CW : HW + (n + 1) * CW] = (hidden_grad * act[part, cols]).astype(BF16)
        for q in range(2):
            begin(gu_copy(1, 2 * h + q))
            begin(gu_copy(3, 2 * h + 1 - q))
        deltas = gu[part, :]
        back = [
            dot(deltas, wgu[c * CW : (c + 1) * CW, :], 1, 1).astype(BF16) for c in range(CB)
        ]
        for g in range(2):
            j = 2 * h + g
            s_b[j * GROUP : (j + 1) * GROUP, :] = pack(
                [block[g * ROWS : (g + 1) * ROWS, :] for block in back]
            )
            start_group(s_b, r_b, sb_sem, rb_sem, j, -1)
        if h == 0:
            pass_on(hid_copy, 0)
        else:
            pass_on(gu_copy, 0)

    def z_copy(n):
        return pltpu.make_async_remote_copy(
            src_ref=z_s.at[n],
            dst_ref=got_hbm.at[n],
            send_sem=zz_s.at[n],
            recv_sem=zz_r.at[n],
            device_id=(partner, me),
            device_id_type=MESH,
        )

    def sums(slices, mine, b, right):
        total = dot(mine[b * NY + y], right(0), 0, 0)
        for k in range(1, NY):
            total = total + dot(slices[k, b], right(k), 0, 0)
        return total

    def hid_of(k):
        return hid[...] if k == 0 else dh[k]

    def gate_of(k):
        return gu[:, :HW] if k == 0 else dgu[k, :, :HW]

    def up_of(k):
        return gu[:, HW:] if k == 0 else dgu[k, :, HW:]

    def send_sums(n, slices, mine, right):
        z_s[n] = sums(slices, mine, 1 - zl, right).astype(BF16)
        begin(z_copy(n))

    def out_copy(n):
        return pltpu.make_async_copy(own.at[n], own_hbm.at[n], osem.at[n])

    def keep_sums(n, slices, mine, right):
        own[n] = sums(slices, mine, zl, right)
        out_copy(n).start()

    wait_slices(a_s, ss, ys_s, ys_r)
    for k, q in ((1, 1), (3, 0), (2, 0), (2, 1)):
        hid_copy(k, q).wait_recv()
    send_sums(2, ss, a_s, hid_of)
    pass_on(gu_copy, 2)
    keep_sums(2, ss, a_s, hid_of)

    wait_slices(a_x, xs, yx_s, yx_r)
    for k, q in ((1, 1), (3, 0), (1, 3), (3, 2), (2, 0), (2, 1), (2, 2), (2, 3)):
        gu_copy(k, q).wait_recv()
    send_sums(0, xs, a_x, gate_of)
    send_sums(1, xs, a_x, up_of)
    keep_sums(0, xs, a_x, gate_of)
    keep_sums(1, xs, a_x, up_of)

    for j in range(NX):
        wait_group(s_b, r_b, sb_sem, rb_sem, j, -1)
        unpack(r_b, a_b, j)
    for c in range(CB):
        xg[:, c * CW : (c + 1) * CW] = dot(pick[...], a_b[c], 0, 0).astype(BF16)
    x_copy = pltpu.make_async_copy(xg, xg_hbm, osem.at[3])
    x_copy.start()
    for n in (2, 0, 1):
        out_copy(n).wait()
    x_copy.wait()
    for copy in sent:
        copy.wait_send()
    for n in (2, 0, 1):
        z_copy(n).wait_recv()


def finish(xg_in, own_in, got_in, xg_out, g_out, u_out, d_out, xv, own, got, isem, osem):
    loads = [
        (
            pltpu.make_async_copy(own_in.at[n], own.at[n], isem.at[n]),
            pltpu.make_async_copy(got_in.at[n], got.at[n], isem.at[3 + n]),
        )
        for n in range(3)
    ]
    x_load = pltpu.make_async_copy(xg_in, xv, isem.at[6])
    for a, b in loads:
        a.start()
        b.start()
    x_load.start()
    stores = []
    for n, out in enumerate((g_out, u_out, d_out)):
        for load in loads[n]:
            load.wait()
        own[n] += got[n].astype(F32)
        stores.append(pltpu.make_async_copy(own.at[n], out, osem.at[n]))
        stores[-1].start()
    x_load.wait()
    stores.append(pltpu.make_async_copy(xv, xg_out, osem.at[3]))
    stores[-1].start()
    for store in stores:
        store.wait()


def on_device(x_tokens, dy_tokens, probs, ids, w_gate, w_up, w_down):
    r = np.arange(GROUP)
    c, rest = r // ROWS, r % ROWS
    tgt = (rest // CAP) * CHUNK + c * CAP + rest % CAP
    inv = np.argsort(tgt)
    vmem = pl.BlockSpec(memory_space=pltpu.VMEM)
    anywhere = pl.BlockSpec(memory_space=pl.ANY)
    dma = pltpu.SemaphoreType.DMA
    grad = jax.ShapeDtypeStruct((D // 8, HW), F32)
    chunks = pltpu.VMEM((NX * GROUP, CW), BF16)
    slots = pltpu.VMEM((CB, SLOTS, CW), BF16)
    x_grad = jax.ShapeDtypeStruct((TOK, D), BF16)
    thirds = (3, D // 8, HW)
    parts = pl.pallas_call(
        kernel,
        out_shape=(
            x_grad,
            jax.ShapeDtypeStruct(thirds, F32),
            jax.ShapeDtypeStruct(thirds, BF16),
        ),
        in_specs=[vmem] * 6 + [anywhere] * 3,
        out_specs=[anywhere] * 3,
        scratch_shapes=[
            pltpu.VMEM((D, 2 * HW), BF16),
            pltpu.VMEM((D, HW), BF16),
            pltpu.VMEM((SLOTS, TOK), BF16),
            pltpu.VMEM((SLOTS, TOK), BF16),
            pltpu.VMEM((GROUP, GROUP), BF16),
            pltpu.VMEM((GROUP, GROUP), BF16),
        ]
        + [chunks] * 6
        + [slots] * 3
        + [
            pltpu.VMEM((SLOTS, HW), F32),
            pltpu.VMEM((SLOTS, HW), F32),
            pltpu.VMEM((SLOTS, HW), BF16),
            pltpu.VMEM((SLOTS, 2 * HW), BF16),
            pltpu.VMEM((NY, 2, SLOTS, CW), BF16),
            pltpu.VMEM((NY, 2, SLOTS, CW), BF16),
            pltpu.VMEM((NY, SLOTS, HW), BF16),
            pltpu.VMEM((NY, SLOTS, 2 * HW), BF16),
            pltpu.VMEM(thirds, BF16),
            pltpu.VMEM(thirds, F32),
            pltpu.VMEM((TOK, D), BF16),
            dma((3,)),
            dma((4,)),
        ]
        + [dma((NX * ZC,))] * 6
        + [dma((4 * NY,))] * 4
        + [dma((2 * NY,))] * 2
        + [dma((4 * NY,))] * 2
        + [dma((3,))] * 2,
        compiler_params=pltpu.CompilerParams(
            collective_id=0, has_side_effects=True, vmem_limit_bytes=60 << 20
        ),
    )(
        ids.T,
        probs.T,
        jnp.asarray(tgt, jnp.int32)[None],
        jnp.asarray(inv, jnp.int32)[None],
        x_tokens,
        dy_tokens,
        w_gate,
        w_up,
        w_down,
    )
    x_grad, gate_grad, up_grad, down_grad = pl.pallas_call(
        finish,
        out_shape=(x_grad, grad, grad, grad),
        in_specs=[anywhere] * 3,
        out_specs=[anywhere] * 4,
        scratch_shapes=[
            pltpu.VMEM((TOK, D), BF16),
            pltpu.VMEM(thirds, F32),
            pltpu.VMEM(thirds, BF16),
            dma((7,)),
            dma((4,)),
        ],
    )(*parts)
    return (x_grad, gate_grad[None], up_grad[None], down_grad[None])


def solution(mesh):
    rows = P(("dp", "expert"), None)
    held = P("expert", None, None)
    owned = P("expert", "dp", None)
    return jax.shard_map(
        on_device,
        mesh=mesh,
        in_specs=(rows, rows, rows, rows, held, held, held),
        out_specs=(rows, owned, owned, owned),
        check_vma=False,
    )
```

```python
import functools

import jax
import jax.numpy as jnp
import numpy as np
from jax import lax
from jax.experimental import pallas as pl
from jax.experimental.pallas import tpu as pltpu
from jax.sharding import PartitionSpec as P

MESH = pl.DeviceIdType.MESH
F32, BF16 = jnp.float32, jnp.bfloat16
CAP = 10
TOK = 128
D = 2048
HW = 768
NX = 4
ZC = 8
NY = 4
CB = 8
CW = D // CB
ROWS = ZC * CAP
CHUNK = CB * CAP
GROUP = ZC * CHUNK
SLOTS = NX * ROWS
AHEAD = 3


def dot(a, b, ca=1, cb=0):
    return lax.dot_general(a, b, (((ca,), (cb,)), ((), ())), preferred_element_type=F32)


def kernel(
    ids_ref, p_ref, tgt_ref, inv_ref, x_ref, dy_ref, wg_hbm, wu_hbm, wd_hbm,
    xg_hbm, own_hbm, got_hbm,
    wgu, wd, pick, pickp, toa, tos,
    s_x, r_x, s_s, r_s, s_b, r_b, a_x, a_s, a_b,
    act, gfac, hid, gu, xs, ss, dh, dgu, z_s, own, xg,
    wsem, osem, sx_sem, rx_sem, sd_sem, rd_sem, sb_sem, rb_sem,
    yx_s, yx_r, ys_s, ys_r, yh_s, yh_r, yg_s, yg_r, zz_s, zz_r,
):
    dpi = lax.axis_index("dp")
    me = lax.axis_index("expert")
    zl, y = dpi // NY, lax.rem(dpi, NY)
    xi, zc = me // ZC, lax.rem(me, ZC)

    loads = [
        pltpu.make_async_copy(wg_hbm.at[0], wgu.at[:, pl.ds(0, HW)], wsem.at[0]),
        pltpu.make_async_copy(wu_hbm.at[0], wgu.at[:, pl.ds(HW, HW)], wsem.at[1]),
        pltpu.make_async_copy(wd_hbm.at[0], wd, wsem.at[2]),
    ]
    for load in loads:
        load.start()

    barrier = pltpu.get_barrier_semaphore()
    for k in range(1, NX * ZC):
        pl.semaphore_signal(
            barrier, inc=1, device_id=(dpi, lax.rem(me + k, NX * ZC)), device_id_type=MESH
        )
    for k in range(1, NY):
        pl.semaphore_signal(
            barrier, inc=1, device_id=(zl * NY + lax.rem(y + k, NY), me), device_id_type=MESH
        )
    partner = (1 - zl) * NY + y
    pl.semaphore_signal(barrier, inc=1, device_id=(partner, me), device_id_type=MESH)

    row = lax.broadcasted_iota(jnp.int32, (NX * ZC, TOK), 0)
    expert = row + ZC * xi
    expert = jnp.where(expert >= NX * ZC, expert - NX * ZC, expert)
    member = jnp.zeros((NX * ZC, TOK), F32)
    weight = jnp.zeros((NX * ZC, TOK), F32)
    probs = p_ref[...].astype(F32)
    for k in range(8):
        same = ids_ref[k : k + 1, :] == expert
        member = jnp.where(same, 1.0, member)
        weight = jnp.where(same, probs[k : k + 1, :], weight)
    before = lax.broadcasted_iota(jnp.int32, (TOK, TOK), 0) < lax.broadcasted_iota(
        jnp.int32, (TOK, TOK), 1
    )
    rank = dot(member.astype(BF16), jnp.where(before, 1.0, 0.0).astype(BF16))
    rank = jnp.where(member > 0.5, rank, -1.0).astype(BF16)
    slot = lax.broadcasted_iota(jnp.int32, (SLOTS, NX * ZC), 0)
    first = CAP * lax.broadcasted_iota(jnp.int32, (SLOTS, NX * ZC), 1)
    spread = jnp.where((slot >= first) & (slot < first + CAP), 1.0, 0.0).astype(BF16)
    of_rank = dot(spread, rank)
    of_weight = dot(spread, weight.astype(BF16))
    of_row = dot(spread, row.astype(F32).astype(BF16))
    place = lax.broadcasted_iota(jnp.int32, (SLOTS, TOK), 0).astype(F32) - CAP * of_row
    hit = of_rank == place
    pick[...] = jnp.where(hit, 1.0, 0.0).astype(BF16)
    pickp[...] = jnp.where(hit, of_weight, 0.0).astype(BF16)
    down = lax.broadcasted_iota(jnp.int32, (GROUP, GROUP), 0)
    tos[...] = jnp.where(down == tgt_ref[...], 1.0, 0.0).astype(BF16)
    toa[...] = jnp.where(down == inv_ref[...], 1.0, 0.0).astype(BF16)

    def exchange(src, dst, send, recv, j, i, sign):
        zt = lax.rem(zc + i, ZC)
        xt = lax.rem(xi + sign * j + NX, NX)
        from_rows = pl.ds(pl.multiple_of((j * ZC + zt) * CHUNK, 16), CHUNK)
        to_rows = pl.ds(pl.multiple_of((j * ZC + zc) * CHUNK, 16), CHUNK)
        if i == 0 and j == 0:
            return pltpu.make_async_copy(src.at[from_rows], dst.at[to_rows], recv.at[0])
        return pltpu.make_async_remote_copy(
            src_ref=src.at[from_rows],
            dst_ref=dst.at[to_rows],
            send_sem=send.at[j * ZC + i],
            recv_sem=recv.at[j * ZC + i],
            device_id=(dpi, xt * ZC + zt),
            device_id_type=MESH,
        )

    sent = []

    def start_group(src, dst, send, recv, j, sign):
        for i in range(ZC):
            copy = exchange(src, dst, send, recv, j, i, sign)
            copy.start()
            if i or j:
                sent.append(copy)

    def wait_group(src, dst, send, recv, j, sign):
        for i in range(ZC):
            copy = exchange(src, dst, send, recv, j, i, sign)
            if i or j:
                copy.wait_recv()
            else:
                copy.wait()

    def pack(blocks):
        return dot(tos[...], jnp.concatenate(blocks, axis=0)).astype(BF16)

    def unpack(src, dst, j):
        rows = dot(toa[...], src[j * GROUP : (j + 1) * GROUP, :]).astype(BF16)
        for c in range(CB):
            dst[c, j * ROWS : (j + 1) * ROWS, :] = rows[c * ROWS : (c + 1) * ROWS, :]

    def gather(sel, tokens, dst, j):
        rows = dot(sel[j * ROWS : (j + 1) * ROWS, :], tokens[...]).astype(BF16)
        dst[j * GROUP : (j + 1) * GROUP, :] = pack(
            [rows[:, c * CW : (c + 1) * CW] for c in range(CB)]
        )

    def start_out(n):
        if n % 2 == 0 and n < 2 * NX:
            start_group(s_x, r_x, sx_sem, rx_sem, n // 2, 1)
        elif n < 2 * NX:
            start_group(s_s, r_s, sd_sem, rd_sem, n // 2, 1)

    for n in range(2 * NX):
        if n % 2 == 0:
            gather(pick, x_ref, s_x, n // 2)
        else:
            gather(pickp, dy_ref, s_s, n // 2)
        if n == 0:
            pl.semaphore_wait(barrier, NX * ZC - 1 + NY)
        if n < AHEAD:
            start_out(n)

    def to_y(src, dst, send, recv, k):
        return pltpu.make_async_remote_copy(
            src_ref=src,
            dst_ref=dst,
            send_sem=send,
            recv_sem=recv,
            device_id=(zl * NY + lax.rem(y + k, NY), me),
            device_id_type=MESH,
        )

    def slice_copy(src, dst, send, recv, k, b, j):
        part = pl.ds(j * ROWS, ROWS)
        n = ((k - 1) * 2 + b) * NX + j
        yt = lax.rem(y + k, NY)
        return to_y(
            src.at[b * NY + yt, part], dst.at[k, b, part], send.at[n], recv.at[n], k
        )

    def start_slices(src, dst, send, recv, j):
        for k in range(1, NY):
            for b in range(2):
                copy = slice_copy(src, dst, send, recv, k, b, j)
                copy.start()
                sent.append(copy)

    def wait_slices(src, dst, send, recv):
        for j in range(NX):
            for k in range(1, NY):
                for b in range(2):
                    slice_copy(src, dst, send, recv, k, b, j).wait_recv()

    def piece_copy(src, dst, send, recv, k, q):
        part = pl.ds(q * ROWS, ROWS)
        n = (k - 1) * NX + q
        if k == 2:
            hop = 1 + 2 * (q % 2)
            return to_y(dst.at[hop, part], dst.at[2, part], send.at[n], recv.at[n], hop)
        return to_y(src.at[part], dst.at[k, part], send.at[n], recv.at[n], k)

    def hid_copy(k, q):
        return piece_copy(hid, dh, yh_s, yh_r, k, q)

    def gu_copy(k, q):
        return piece_copy(gu, dgu, yg_s, yg_r, k, q)

    def begin(copy):
        copy.start()
        sent.append(copy)

    def pass_on(piece, q):
        piece(1 + 2 * (q % 2), q).wait_recv()
        begin(piece(2, q))

    def start_piece(piece, q):
        begin(piece(1 + 2 * (q % 2), q))
        begin(piece(3 - 2 * (q % 2), q))

    def start_back(j):
        start_group(s_b, r_b, sb_sem, rb_sem, j, -1)

    for j in range(NX):
        part = slice(j * ROWS, (j + 1) * ROWS)
        wait_group(s_x, r_x, sx_sem, rx_sem, j, 1)
        start_out(2 * j + AHEAD)
        unpack(r_x, a_x, j)
        start_slices(a_x, xs, yx_s, yx_r, j)
        if j == 0:
            for load in loads:
                load.wait()
        rows = jnp.concatenate([a_x[c, part, :] for c in range(CB)], axis=1)
        for n in range(HW // CW):
            cols = slice(n * CW, (n + 1) * CW)
            gate_pre = dot(rows, wgu[:, n * CW : (n + 1) * CW])
            up_pre = dot(rows, wgu[:, HW + n * CW : HW + (n + 1) * CW])
            sig = 1.0 / (1.0 + jnp.exp(-gate_pre))
            gate_act = gate_pre * sig
            act[part, cols] = gate_act
            gfac[part, cols] = up_pre * sig * (1.0 + gate_pre * (1.0 - sig))
            hid[part, cols] = (gate_act * up_pre).astype(BF16)
        if j == NX - 1:
            start_back(0)
        else:
            start_piece(hid_copy, j)
        wait_group(s_s, r_s, sd_sem, rd_sem, j, 1)
        start_out(2 * j + 1 + AHEAD)
        if j == NX - 1:
            start_back(1)
            start_back(2)
        unpack(r_s, a_s, j)
        rows = jnp.concatenate([a_s[c, part, :] for c in range(CB)], axis=1)
        for n in range(HW // CW):
            cols = slice(n * CW, (n + 1) * CW)
            hidden_grad = dot(rows, wd[:, n * CW : (n + 1) * CW])
            gu[part, cols] = (hidden_grad * gfac[part, cols]).astype(BF16)
            gu[part, HW + n * CW : HW + (n + 1) * CW] = (hidden_grad * act[part, cols]).astype(BF16)
        start_piece(gu_copy, j)
        deltas = gu[part, :]
        s_b[j * GROUP : (j + 1) * GROUP, :] = pack(
            [dot(deltas, wgu[c * CW : (c + 1) * CW, :], 1, 1).astype(BF16) for c in range(CB)]
        )
        if j == NX - 1:
            start_back(j)
        if j > 0:
            pass_on(gu_copy, j - 1)
            if j < NX - 1:
                pass_on(hid_copy, j - 1)
    start_piece(hid_copy, NX - 1)
    pass_on(gu_copy, NX - 1)
    for j in range(NX):
        start_slices(a_s, ss, ys_s, ys_r, j)
        if j > 1:
            pass_on(hid_copy, j)

    def z_copy(n):
        return pltpu.make_async_remote_copy(
            src_ref=z_s.at[n],
            dst_ref=got_hbm.at[n],
            send_sem=zz_s.at[n],
            recv_sem=zz_r.at[n],
            device_id=(partner, me),
            device_id_type=MESH,
        )

    def sums(slices, mine, b, right):
        total = dot(mine[b * NY + y], right(0), 0, 0)
        for k in range(1, NY):
            total = total + dot(slices[k, b], right(k), 0, 0)
        return total

    def hid_of(k):
        return hid[...] if k == 0 else dh[k]

    def gate_of(k):
        return gu[:, :HW] if k == 0 else dgu[k, :, :HW]

    def up_of(k):
        return gu[:, HW:] if k == 0 else dgu[k, :, HW:]

    def send_sums(n, slices, mine, right):
        z_s[n] = sums(slices, mine, 1 - zl, right).astype(BF16)
        begin(z_copy(n))

    def out_copy(n):
        return pltpu.make_async_copy(own.at[n], own_hbm.at[n], osem.at[n])

    def keep_sums(n, slices, mine, right):
        own[n] = sums(slices, mine, zl, right)
        out_copy(n).start()

    def wait_pieces(piece):
        for q in range(NX):
            piece(3 - 2 * (q % 2), q).wait_recv()
            piece(2, q).wait_recv()

    wait_slices(a_x, xs, yx_s, yx_r)
    wait_pieces(gu_copy)
    send_sums(0, xs, a_x, gate_of)
    send_sums(1, xs, a_x, up_of)
    wait_slices(a_s, ss, ys_s, ys_r)
    wait_pieces(hid_copy)
    send_sums(2, ss, a_s, hid_of)
    keep_sums(0, xs, a_x, gate_of)
    keep_sums(1, xs, a_x, up_of)
    keep_sums(2, ss, a_s, hid_of)

    for j in range(NX):
        wait_group(s_b, r_b, sb_sem, rb_sem, j, -1)
        unpack(r_b, a_b, j)
    for c in range(CB):
        xg[:, c * CW : (c + 1) * CW] = dot(pick[...], a_b[c], 0, 0).astype(BF16)
    x_copy = pltpu.make_async_copy(xg, xg_hbm, osem.at[3])
    x_copy.start()
    for n in (2, 0, 1):
        out_copy(n).wait()
    x_copy.wait()
    for copy in sent:
        copy.wait_send()
    for n in (2, 0, 1):
        z_copy(n).wait_recv()


def finish(xg_in, own_in, got_in, xg_out, g_out, u_out, d_out, xv, own, got, isem, osem):
    loads = [
        (
            pltpu.make_async_copy(own_in.at[n], own.at[n], isem.at[n]),
            pltpu.make_async_copy(got_in.at[n], got.at[n], isem.at[3 + n]),
        )
        for n in range(3)
    ]
    x_load = pltpu.make_async_copy(xg_in, xv, isem.at[6])
    for a, b in loads:
        a.start()
        b.start()
    x_load.start()
    stores = []
    for n, out in enumerate((g_out, u_out, d_out)):
        for load in loads[n]:
            load.wait()
        own[n] += got[n].astype(F32)
        stores.append(pltpu.make_async_copy(own.at[n], out, osem.at[n]))
        stores[-1].start()
    x_load.wait()
    stores.append(pltpu.make_async_copy(xv, xg_out, osem.at[3]))
    stores[-1].start()
    for store in stores:
        store.wait()


def on_device(x_tokens, dy_tokens, probs, ids, w_gate, w_up, w_down):
    r = np.arange(GROUP)
    c, rest = r // ROWS, r % ROWS
    tgt = (rest // CAP) * CHUNK + c * CAP + rest % CAP
    inv = np.argsort(tgt)
    vmem = pl.BlockSpec(memory_space=pltpu.VMEM)
    anywhere = pl.BlockSpec(memory_space=pl.ANY)
    dma = pltpu.SemaphoreType.DMA
    grad = jax.ShapeDtypeStruct((D // 8, HW), F32)
    chunks = pltpu.VMEM((NX * GROUP, CW), BF16)
    slots = pltpu.VMEM((CB, SLOTS, CW), BF16)
    x_grad = jax.ShapeDtypeStruct((TOK, D), BF16)
    thirds = (3, D // 8, HW)
    parts = pl.pallas_call(
        kernel,
        out_shape=(
            x_grad,
            jax.ShapeDtypeStruct(thirds, F32),
            jax.ShapeDtypeStruct(thirds, BF16),
        ),
        in_specs=[vmem] * 6 + [anywhere] * 3,
        out_specs=[anywhere] * 3,
        scratch_shapes=[
            pltpu.VMEM((D, 2 * HW), BF16),
            pltpu.VMEM((D, HW), BF16),
            pltpu.VMEM((SLOTS, TOK), BF16),
            pltpu.VMEM((SLOTS, TOK), BF16),
            pltpu.VMEM((GROUP, GROUP), BF16),
            pltpu.VMEM((GROUP, GROUP), BF16),
        ]
        + [chunks] * 6
        + [slots] * 3
        + [
            pltpu.VMEM((SLOTS, HW), F32),
            pltpu.VMEM((SLOTS, HW), F32),
            pltpu.VMEM((SLOTS, HW), BF16),
            pltpu.VMEM((SLOTS, 2 * HW), BF16),
            pltpu.VMEM((NY, 2, SLOTS, CW), BF16),
            pltpu.VMEM((NY, 2, SLOTS, CW), BF16),
            pltpu.VMEM((NY, SLOTS, HW), BF16),
            pltpu.VMEM((NY, SLOTS, 2 * HW), BF16),
            pltpu.VMEM(thirds, BF16),
            pltpu.VMEM(thirds, F32),
            pltpu.VMEM((TOK, D), BF16),
            dma((3,)),
            dma((4,)),
        ]
        + [dma((NX * ZC,))] * 6
        + [dma((6 * NX,))] * 4
        + [dma((3 * NX,))] * 4
        + [dma((3,))] * 2,
        compiler_params=pltpu.CompilerParams(
            collective_id=0, has_side_effects=True, vmem_limit_bytes=60 << 20
        ),
    )(
        ids.T,
        probs.T,
        jnp.asarray(tgt, jnp.int32)[None],
        jnp.asarray(inv, jnp.int32)[None],
        x_tokens,
        dy_tokens,
        w_gate,
        w_up,
        w_down,
    )
    x_grad, gate_grad, up_grad, down_grad = pl.pallas_call(
        finish,
        out_shape=(x_grad, grad, grad, grad),
        in_specs=[anywhere] * 3,
        out_specs=[anywhere] * 4,
        scratch_shapes=[
            pltpu.VMEM((TOK, D), BF16),
            pltpu.VMEM(thirds, F32),
            pltpu.VMEM(thirds, BF16),
            dma((7,)),
            dma((4,)),
        ],
    )(*parts)
    return (x_grad, gate_grad[None], up_grad[None], down_grad[None])


def solution(mesh):
    rows = P(("dp", "expert"), None)
    held = P("expert", None, None)
    owned = P("expert", "dp", None)
    return jax.shard_map(
        on_device,
        mesh=mesh,
        in_specs=(rows, rows, rows, rows, held, held, held),
        out_specs=(rows, owned, owned, owned),
        check_vma=False,
    )
```

```python
import functools

import jax
import jax.numpy as jnp
import numpy as np
from jax import lax
from jax.experimental import pallas as pl
from jax.experimental.pallas import tpu as pltpu
from jax.sharding import PartitionSpec as P

MESH = pl.DeviceIdType.MESH
F32, BF16 = jnp.float32, jnp.bfloat16
CAP = 10
TOK = 128
D = 2048
HW = 768
NX = 4
NZ = 4
ZC = 2 * NZ
NY = 4
CB = 8
CW = D // CB
ROWS = ZC * CAP
CHUNK = CB * CAP
GROUP = ZC * CHUNK
SLOTS = NX * ROWS
AHEAD = 3


def dot(a, b, ca=1, cb=0):
    return lax.dot_general(a, b, (((ca,), (cb,)), ((), ())), preferred_element_type=F32)


def kernel(
    ids_ref, p_ref, tgt_ref, inv_ref, x_ref, dy_ref, wg_hbm, wu_hbm, wd_hbm,
    xg_hbm, own_hbm, got_hbm,
    wgu, wd, pick, pickp, toa, tos,
    s_x, r_x, s_s, r_s, s_b, r_b, a_x, a_s, a_b,
    act, gfac, hid, gu, xs, ss, dh, dgu, z_s, own, xg,
    wsem, osem, sx_sem, rx_sem, sd_sem, rd_sem, sb_sem, rb_sem,
    yx_s, yx_r, ys_s, ys_r, yh_s, yh_r, yg_s, yg_r, zz_s, zz_r,
):
    dpi = lax.axis_index("dp")
    me = lax.axis_index("expert")
    zl, y = dpi // NY, lax.rem(dpi, NY)
    xi, zc = me // ZC, lax.rem(me, ZC)
    zh, core = zc // 2, lax.rem(zc, 2)

    loads = [
        pltpu.make_async_copy(wg_hbm.at[0], wgu.at[:, pl.ds(0, HW)], wsem.at[0]),
        pltpu.make_async_copy(wu_hbm.at[0], wgu.at[:, pl.ds(HW, HW)], wsem.at[1]),
        pltpu.make_async_copy(wd_hbm.at[0], wd, wsem.at[2]),
    ]
    for load in loads:
        load.start()

    barrier = pltpu.get_barrier_semaphore()
    met = ((zl, 0), (zl, 1), (zl, 3), (1 - zl, 2), (1 - zl, 3 - 2 * zl))
    for n, (zlt, far) in enumerate(met):
        for k in range(2 * NX):
            if n or k:
                other = (
                    lax.rem(xi + k // 2, NX) * ZC
                    + lax.rem(zh + far, NZ) * 2
                    + lax.rem(core + k, 2)
                )
                pl.semaphore_signal(
                    barrier, inc=1, device_id=(zlt * NY + y, other), device_id_type=MESH
                )
    for k in range(1, NY):
        pl.semaphore_signal(
            barrier, inc=1, device_id=(zl * NY + lax.rem(y + k, NY), me), device_id_type=MESH
        )
    partner = (1 - zl) * NY + y
    pl.semaphore_signal(barrier, inc=1, device_id=(partner, me), device_id_type=MESH)

    row = lax.broadcasted_iota(jnp.int32, (NX * ZC, TOK), 0)
    expert = row + ZC * xi
    expert = jnp.where(expert >= NX * ZC, expert - NX * ZC, expert)
    member = jnp.zeros((NX * ZC, TOK), F32)
    weight = jnp.zeros((NX * ZC, TOK), F32)
    probs = p_ref[...].astype(F32)
    for k in range(8):
        same = ids_ref[k : k + 1, :] == expert
        member = jnp.where(same, 1.0, member)
        weight = jnp.where(same, probs[k : k + 1, :], weight)
    before = lax.broadcasted_iota(jnp.int32, (TOK, TOK), 0) < lax.broadcasted_iota(
        jnp.int32, (TOK, TOK), 1
    )
    rank = dot(member.astype(BF16), jnp.where(before, 1.0, 0.0).astype(BF16))
    rank = jnp.where(member > 0.5, rank, -1.0).astype(BF16)
    slot = lax.broadcasted_iota(jnp.int32, (SLOTS, NX * ZC), 0)
    first = CAP * lax.broadcasted_iota(jnp.int32, (SLOTS, NX * ZC), 1)
    spread = jnp.where((slot >= first) & (slot < first + CAP), 1.0, 0.0).astype(BF16)
    of_rank = dot(spread, rank)
    of_weight = dot(spread, weight.astype(BF16))
    of_row = dot(spread, row.astype(F32).astype(BF16))
    place = lax.broadcasted_iota(jnp.int32, (SLOTS, TOK), 0).astype(F32) - CAP * of_row
    hit = of_rank == place
    pick[...] = jnp.where(hit, 1.0, 0.0).astype(BF16)
    pickp[...] = jnp.where(hit, of_weight, 0.0).astype(BF16)
    down = lax.broadcasted_iota(jnp.int32, (GROUP, GROUP), 0)
    tos[...] = jnp.where(down == tgt_ref[...], 1.0, 0.0).astype(BF16)
    toa[...] = jnp.where(down == inv_ref[...], 1.0, 0.0).astype(BF16)

    def exchange(src, dst, send, recv, j, i, sign):
        far, flip = i // 2, i % 2
        ct = lax.rem(core + flip, 2)
        xt = lax.rem(xi + sign * j + NX, NX)
        if sign > 0:
            zt = lax.rem(zh + far, NZ)
            zlt = (zl, 0, 1 - zl, 1)[far]
            take = zt * 2 + ct
            spot = (0, 1 + 2 * zl, 2, 1 + 2 * zl)[far]
            put = spot * 2 + core
        else:
            zt = lax.rem(zh + (0, 3 - 2 * zl, 2, 3 - 2 * zl)[far], NZ)
            zlt = (zl, 0, 1 - zl, 1)[far]
            take = far * 2 + ct
            spot = (0, 1 + 2 * zl, 2, 1 + 2 * zl)[far]
            put = zc
        from_rows = pl.ds(pl.multiple_of((j * ZC + take) * CHUNK, 16), CHUNK)
        to_rows = pl.ds(pl.multiple_of((j * ZC + put) * CHUNK, 16), CHUNK)
        if i == 0 and j == 0:
            return pltpu.make_async_copy(src.at[from_rows], dst.at[to_rows], recv.at[0])
        return pltpu.make_async_remote_copy(
            src_ref=src.at[from_rows],
            dst_ref=dst.at[to_rows],
            send_sem=send.at[j * ZC + i],
            recv_sem=recv.at[j * ZC + spot * 2 + flip],
            device_id=(zlt * NY + y, xt * ZC + zt * 2 + ct),
            device_id_type=MESH,
        )

    def arrival(src, dst, send, recv, j, i):
        rows = pl.ds((j * ZC + i) * CHUNK, CHUNK)
        return pltpu.make_async_remote_copy(
            src_ref=src.at[rows],
            dst_ref=dst.at[rows],
            send_sem=send.at[j * ZC + i],
            recv_sem=recv.at[j * ZC + i],
            device_id=(partner, me),
            device_id_type=MESH,
        )

    sent = []

    def start_group(src, dst, send, recv, j, sign):
        for i in range(ZC):
            copy = exchange(src, dst, send, recv, j, i, sign)
            copy.start()
            if i or j:
                sent.append(copy)

    def wait_group(src, dst, send, recv, j, sign):
        for i in range(ZC):
            if i or j:
                arrival(src, dst, send, recv, j, i).wait_recv()
            else:
                exchange(src, dst, send, recv, j, i, sign).wait()

    def pack(blocks):
        return dot(tos[...], jnp.concatenate(blocks, axis=0)).astype(BF16)

    def unpack(src, dst, j):
        rows = dot(toa[...], src[j * GROUP : (j + 1) * GROUP, :]).astype(BF16)
        for c in range(CB):
            dst[c, j * ROWS : (j + 1) * ROWS, :] = rows[c * ROWS : (c + 1) * ROWS, :]

    def gather(sel, tokens, dst, j):
        rows = dot(sel[j * ROWS : (j + 1) * ROWS, :], tokens[...]).astype(BF16)
        dst[j * GROUP : (j + 1) * GROUP, :] = pack(
            [rows[:, c * CW : (c + 1) * CW] for c in range(CB)]
        )

    def start_out(n):
        if n % 2 == 0 and n < 2 * NX:
            start_group(s_x, r_x, sx_sem, rx_sem, n // 2, 1)
        elif n < 2 * NX:
            start_group(s_s, r_s, sd_sem, rd_sem, n // 2, 1)

    for n in range(2 * NX):
        if n % 2 == 0:
            gather(pick, x_ref, s_x, n // 2)
        else:
            gather(pickp, dy_ref, s_s, n // 2)
        if n == 0:
            pl.semaphore_wait(barrier, 10 * NX - 1 + NY)
        if n < AHEAD:
            start_out(n)

    def to_y(src, dst, send, recv, k):
        return pltpu.make_async_remote_copy(
            src_ref=src,
            dst_ref=dst,
            send_sem=send,
            recv_sem=recv,
            device_id=(zl * NY + lax.rem(y + k, NY), me),
            device_id_type=MESH,
        )

    def block_of(b):
        return zl if b else 1 - zl

    def slice_copy(src, dst, send, recv, k, b, j):
        part = pl.ds(j * ROWS, ROWS)
        n = ((k - 1) * 2 + b) * NX + j
        yt = lax.rem(y + k, NY)
        return to_y(
            src.at[block_of(b) * NY + yt, part], dst.at[k, b, part], send.at[n], recv.at[n], k
        )

    def start_slices(src, dst, send, recv, j, b):
        for k in range(1, NY):
            copy = slice_copy(src, dst, send, recv, k, b, j)
            copy.start()
            sent.append(copy)

    def wait_slices(src, dst, send, recv, b):
        for j in range(NX):
            for k in range(1, NY):
                slice_copy(src, dst, send, recv, k, b, j).wait_recv()

    def piece_copy(src, dst, send, recv, k, q):
        part = pl.ds(q * ROWS, ROWS)
        n = (k - 1) * NX + q
        if k == 2:
            hop = 1 + 2 * (q % 2)
            return to_y(dst.at[hop, part], dst.at[2, part], send.at[n], recv.at[n], hop)
        return to_y(src.at[part], dst.at[k, part], send.at[n], recv.at[n], k)

    def hid_copy(k, q):
        return piece_copy(hid, dh, yh_s, yh_r, k, q)

    def gu_copy(k, q):
        return piece_copy(gu, dgu, yg_s, yg_r, k, q)

    def begin(copy):
        copy.start()
        sent.append(copy)

    def pass_on(piece, q):
        piece(1 + 2 * (q % 2), q).wait_recv()
        begin(piece(2, q))

    def start_piece(piece, q):
        begin(piece(1 + 2 * (q % 2), q))
        begin(piece(3 - 2 * (q % 2), q))

    def start_back(j):
        start_group(s_b, r_b, sb_sem, rb_sem, j, -1)

    for j in range(NX):
        part = slice(j * ROWS, (j + 1) * ROWS)
        wait_group(s_x, r_x, sx_sem, rx_sem, j, 1)
        start_out(2 * j + AHEAD)
        unpack(r_x, a_x, j)
        start_slices(a_x, xs, yx_s, yx_r, j, 0)
        if j == 0:
            for load in loads:
                load.wait()
        rows = jnp.concatenate([a_x[c, part, :] for c in range(CB)], axis=1)
        for n in range(HW // CW):
            cols = slice(n * CW, (n + 1) * CW)
            gate_pre = dot(rows, wgu[:, n * CW : (n + 1) * CW])
            up_pre = dot(rows, wgu[:, HW + n * CW : HW + (n + 1) * CW])
            sig = 1.0 / (1.0 + jnp.exp(-gate_pre))
            gate_act = gate_pre * sig
            act[part, cols] = gate_act
            gfac[part, cols] = up_pre * sig * (1.0 + gate_pre * (1.0 - sig))
            hid[part, cols] = (gate_act * up_pre).astype(BF16)
        start_piece(hid_copy, j)
        if j == NX - 1:
            start_back(0)
        wait_group(s_s, r_s, sd_sem, rd_sem, j, 1)
        start_out(2 * j + 1 + AHEAD)
        if j == NX - 1:
            start_back(1)
            start_back(2)
        unpack(r_s, a_s, j)
        rows = jnp.concatenate([a_s[c, part, :] for c in range(CB)], axis=1)
        for n in range(HW // CW):
            cols = slice(n * CW, (n + 1) * CW)
            hidden_grad = dot(rows, wd[:, n * CW : (n + 1) * CW])
            gu[part, cols] = (hidden_grad * gfac[part, cols]).astype(BF16)
            gu[part, HW + n * CW : HW + (n + 1) * CW] = (hidden_grad * act[part, cols]).astype(BF16)
        start_slices(a_s, ss, ys_s, ys_r, j, 0)
        start_piece(gu_copy, j)
        deltas = gu[part, :]
        s_b[j * GROUP : (j + 1) * GROUP, :] = pack(
            [dot(deltas, wgu[c * CW : (c + 1) * CW, :], 1, 1).astype(BF16) for c in range(CB)]
        )
        if j == NX - 1:
            start_back(j)
        if j > 0:
            pass_on(gu_copy, j - 1)
            pass_on(hid_copy, j - 1)
    pass_on(hid_copy, NX - 1)

    def z_copy(n):
        return pltpu.make_async_remote_copy(
            src_ref=z_s.at[n],
            dst_ref=got_hbm.at[n],
            send_sem=zz_s.at[n],
            recv_sem=zz_r.at[n],
            device_id=(partner, me),
            device_id_type=MESH,
        )

    def sums(slices, mine, b, right):
        total = dot(mine[block_of(b) * NY + y], right(0), 0, 0)
        for k in range(1, NY):
            total = total + dot(slices[k, b], right(k), 0, 0)
        return total

    def hid_of(k):
        return hid[...] if k == 0 else dh[k]

    def gate_of(k):
        return gu[:, :HW] if k == 0 else dgu[k, :, :HW]

    def up_of(k):
        return gu[:, HW:] if k == 0 else dgu[k, :, HW:]

    def send_sums(n, slices, mine, right):
        z_s[n] = sums(slices, mine, 0, right).astype(BF16)
        begin(z_copy(n))

    def out_copy(n):
        return pltpu.make_async_copy(own.at[n], own_hbm.at[n], osem.at[n])

    def keep_sums(n, slices, mine, right):
        own[n] = sums(slices, mine, 1, right)
        out_copy(n).start()

    def wait_pieces(piece):
        for q in range(NX):
            piece(3 - 2 * (q % 2), q).wait_recv()
            piece(2, q).wait_recv()

    pass_on(gu_copy, NX - 1)
    for j in range(NX):
        start_slices(a_s, ss, ys_s, ys_r, j, 1)
        start_slices(a_x, xs, yx_s, yx_r, j, 1)
    wait_slices(a_s, ss, ys_s, ys_r, 0)
    wait_pieces(hid_copy)
    send_sums(2, ss, a_s, hid_of)
    wait_slices(a_x, xs, yx_s, yx_r, 0)
    wait_pieces(gu_copy)
    send_sums(0, xs, a_x, gate_of)
    send_sums(1, xs, a_x, up_of)

    for j in range(NX):
        wait_group(s_b, r_b, sb_sem, rb_sem, j, -1)
        unpack(r_b, a_b, j)
    for c in range(CB):
        xg[:, c * CW : (c + 1) * CW] = dot(pick[...], a_b[c], 0, 0).astype(BF16)
    wait_slices(a_s, ss, ys_s, ys_r, 1)
    keep_sums(2, ss, a_s, hid_of)
    wait_slices(a_x, xs, yx_s, yx_r, 1)
    keep_sums(0, xs, a_x, gate_of)
    keep_sums(1, xs, a_x, up_of)
    x_copy = pltpu.make_async_copy(xg, xg_hbm, osem.at[3])
    x_copy.start()
    for n in (2, 0, 1):
        out_copy(n).wait()
    x_copy.wait()
    for copy in sent:
        copy.wait_send()
    for n in (2, 0, 1):
        z_copy(n).wait_recv()


def finish(xg_in, own_in, got_in, xg_out, g_out, u_out, d_out, xv, own, got, isem, osem):
    loads = [
        (
            pltpu.make_async_copy(own_in.at[n], own.at[n], isem.at[n]),
            pltpu.make_async_copy(got_in.at[n], got.at[n], isem.at[3 + n]),
        )
        for n in range(3)
    ]
    x_load = pltpu.make_async_copy(xg_in, xv, isem.at[6])
    for a, b in loads:
        a.start()
        b.start()
    x_load.start()
    stores = []
    for n, out in enumerate((g_out, u_out, d_out)):
        for load in loads[n]:
            load.wait()
        own[n] += got[n].astype(F32)
        stores.append(pltpu.make_async_copy(own.at[n], out, osem.at[n]))
        stores[-1].start()
    x_load.wait()
    stores.append(pltpu.make_async_copy(xv, xg_out, osem.at[3]))
    stores[-1].start()
    for store in stores:
        store.wait()


def on_device(x_tokens, dy_tokens, probs, ids, w_gate, w_up, w_down):
    r = np.arange(GROUP)
    c, rest = r // ROWS, r % ROWS
    tgt = (rest // CAP) * CHUNK + c * CAP + rest % CAP
    inv = np.argsort(tgt)
    vmem = pl.BlockSpec(memory_space=pltpu.VMEM)
    anywhere = pl.BlockSpec(memory_space=pl.ANY)
    dma = pltpu.SemaphoreType.DMA
    grad = jax.ShapeDtypeStruct((D // 8, HW), F32)
    chunks = pltpu.VMEM((NX * GROUP, CW), BF16)
    slots = pltpu.VMEM((CB, SLOTS, CW), BF16)
    x_grad = jax.ShapeDtypeStruct((TOK, D), BF16)
    thirds = (3, D // 8, HW)
    parts = pl.pallas_call(
        kernel,
        out_shape=(
            x_grad,
            jax.ShapeDtypeStruct(thirds, F32),
            jax.ShapeDtypeStruct(thirds, BF16),
        ),
        in_specs=[vmem] * 6 + [anywhere] * 3,
        out_specs=[anywhere] * 3,
        scratch_shapes=[
            pltpu.VMEM((D, 2 * HW), BF16),
            pltpu.VMEM((D, HW), BF16),
            pltpu.VMEM((SLOTS, TOK), BF16),
            pltpu.VMEM((SLOTS, TOK), BF16),
            pltpu.VMEM((GROUP, GROUP), BF16),
            pltpu.VMEM((GROUP, GROUP), BF16),
        ]
        + [chunks] * 6
        + [slots] * 3
        + [
            pltpu.VMEM((SLOTS, HW), F32),
            pltpu.VMEM((SLOTS, HW), F32),
            pltpu.VMEM((SLOTS, HW), BF16),
            pltpu.VMEM((SLOTS, 2 * HW), BF16),
            pltpu.VMEM((NY, 2, SLOTS, CW), BF16),
            pltpu.VMEM((NY, 2, SLOTS, CW), BF16),
            pltpu.VMEM((NY, SLOTS, HW), BF16),
            pltpu.VMEM((NY, SLOTS, 2 * HW), BF16),
            pltpu.VMEM(thirds, BF16),
            pltpu.VMEM(thirds, F32),
            pltpu.VMEM((TOK, D), BF16),
            dma((3,)),
            dma((4,)),
        ]
        + [dma((NX * ZC,))] * 6
        + [dma((6 * NX,))] * 4
        + [dma((3 * NX,))] * 4
        + [dma((3,))] * 2,
        compiler_params=pltpu.CompilerParams(
            collective_id=0, has_side_effects=True, vmem_limit_bytes=60 << 20
        ),
    )(
        ids.T,
        probs.T,
        jnp.asarray(tgt, jnp.int32)[None],
        jnp.asarray(inv, jnp.int32)[None],
        x_tokens,
        dy_tokens,
        w_gate,
        w_up,
        w_down,
    )
    x_grad, gate_grad, up_grad, down_grad = pl.pallas_call(
        finish,
        out_shape=(x_grad, grad, grad, grad),
        in_specs=[anywhere] * 3,
        out_specs=[anywhere] * 4,
        scratch_shapes=[
            pltpu.VMEM((TOK, D), BF16),
            pltpu.VMEM(thirds, F32),
            pltpu.VMEM(thirds, BF16),
            dma((7,)),
            dma((4,)),
        ],
    )(*parts)
    return (x_grad, gate_grad[None], up_grad[None], down_grad[None])


def solution(mesh):
    rows = P(("dp", "expert"), None)
    held = P("expert", None, None)
    owned = P("expert", "dp", None)
    return jax.shard_map(
        on_device,
        mesh=mesh,
        in_specs=(rows, rows, rows, rows, held, held, held),
        out_specs=(rows, owned, owned, owned),
        check_vma=False,
    )
```

```python
import functools

import jax
import jax.numpy as jnp
import numpy as np
from jax import lax
from jax.experimental import pallas as pl
from jax.experimental.pallas import tpu as pltpu
from jax.sharding import PartitionSpec as P

MESH = pl.DeviceIdType.MESH
F32, BF16 = jnp.float32, jnp.bfloat16
CAP = 10
TOK = 128
D = 2048
HW = 768
NX = 4
NZ = 4
ZC = 2 * NZ
NY = 4
CB = 8
CW = D // CB
ROWS = ZC * CAP
CHUNK = CB * CAP
GROUP = ZC * CHUNK
SLOTS = NX * ROWS
AHEAD = 3


def dot(a, b, ca=1, cb=0):
    return lax.dot_general(a, b, (((ca,), (cb,)), ((), ())), preferred_element_type=F32)


def kernel(
    ids_ref, p_ref, tgt_ref, inv_ref, x_ref, dy_ref, wg_hbm, wu_hbm, wd_hbm,
    xg_hbm, own_hbm, got_hbm,
    wgu, wd, pick, pickp, toa, tos,
    s_x, r_x, s_s, r_s, s_b, r_b, a_x, a_s, a_b,
    act, gfac, hid, gu, xs, ss, dh, dgu, z_s, own, xg,
    wsem, osem, sx_sem, rx_sem, sd_sem, rd_sem, sb_sem, rb_sem,
    yx_s, yx_r, ys_s, ys_r, yh_s, yh_r, yg_s, yg_r, yu_s, yu_r, zz_s, zz_r,
):
    dpi = lax.axis_index("dp")
    me = lax.axis_index("expert")
    zl, y = dpi // NY, lax.rem(dpi, NY)
    xi, zc = me // ZC, lax.rem(me, ZC)
    zh, core = zc // 2, lax.rem(zc, 2)

    loads = [
        pltpu.make_async_copy(wg_hbm.at[0], wgu.at[:, pl.ds(0, HW)], wsem.at[0]),
        pltpu.make_async_copy(wu_hbm.at[0], wgu.at[:, pl.ds(HW, HW)], wsem.at[1]),
        pltpu.make_async_copy(wd_hbm.at[0], wd, wsem.at[2]),
    ]
    for load in loads:
        load.start()

    barrier = pltpu.get_barrier_semaphore()
    met = ((zl, 0), (zl, 1), (zl, 3), (1 - zl, 2), (1 - zl, 3 - 2 * zl))
    for n, (zlt, far) in enumerate(met):
        for k in range(2 * NX):
            if n or k:
                other = (
                    lax.rem(xi + k // 2, NX) * ZC
                    + lax.rem(zh + far, NZ) * 2
                    + lax.rem(core + k, 2)
                )
                pl.semaphore_signal(
                    barrier, inc=1, device_id=(zlt * NY + y, other), device_id_type=MESH
                )
    for k in range(1, NY):
        pl.semaphore_signal(
            barrier, inc=1, device_id=(zl * NY + lax.rem(y + k, NY), me), device_id_type=MESH
        )
    partner = (1 - zl) * NY + y
    pl.semaphore_signal(barrier, inc=1, device_id=(partner, me), device_id_type=MESH)

    row = lax.broadcasted_iota(jnp.int32, (NX * ZC, TOK), 0)
    expert = row + ZC * xi
    expert = jnp.where(expert >= NX * ZC, expert - NX * ZC, expert)
    member = jnp.zeros((NX * ZC, TOK), F32)
    weight = jnp.zeros((NX * ZC, TOK), F32)
    probs = p_ref[...].astype(F32)
    for k in range(8):
        same = ids_ref[k : k + 1, :] == expert
        member = jnp.where(same, 1.0, member)
        weight = jnp.where(same, probs[k : k + 1, :], weight)
    before = lax.broadcasted_iota(jnp.int32, (TOK, TOK), 0) < lax.broadcasted_iota(
        jnp.int32, (TOK, TOK), 1
    )
    rank = dot(member.astype(BF16), jnp.where(before, 1.0, 0.0).astype(BF16))
    rank = jnp.where(member > 0.5, rank, -1.0).astype(BF16)
    slot = lax.broadcasted_iota(jnp.int32, (SLOTS, NX * ZC), 0)
    first = CAP * lax.broadcasted_iota(jnp.int32, (SLOTS, NX * ZC), 1)
    spread = jnp.where((slot >= first) & (slot < first + CAP), 1.0, 0.0).astype(BF16)
    of_rank = dot(spread, rank)
    of_weight = dot(spread, weight.astype(BF16))
    of_row = dot(spread, row.astype(F32).astype(BF16))
    place = lax.broadcasted_iota(jnp.int32, (SLOTS, TOK), 0).astype(F32) - CAP * of_row
    hit = of_rank == place
    pick[...] = jnp.where(hit, 1.0, 0.0).astype(BF16)
    pickp[...] = jnp.where(hit, of_weight, 0.0).astype(BF16)
    down = lax.broadcasted_iota(jnp.int32, (GROUP, GROUP), 0)
    tos[...] = jnp.where(down == tgt_ref[...], 1.0, 0.0).astype(BF16)
    toa[...] = jnp.where(down == inv_ref[...], 1.0, 0.0).astype(BF16)

    def exchange(src, dst, send, recv, j, i, sign):
        far, flip = i // 2, i % 2
        ct = lax.rem(core + flip, 2)
        xt = lax.rem(xi + sign * j + NX, NX)
        if sign > 0:
            zt = lax.rem(zh + far, NZ)
            zlt = (zl, 0, 1 - zl, 1)[far]
            take = zt * 2 + ct
            spot = (0, 1 + 2 * zl, 2, 1 + 2 * zl)[far]
            put = spot * 2 + core
        else:
            zt = lax.rem(zh + (0, 3 - 2 * zl, 2, 3 - 2 * zl)[far], NZ)
            zlt = (zl, 0, 1 - zl, 1)[far]
            take = far * 2 + ct
            spot = (0, 1 + 2 * zl, 2, 1 + 2 * zl)[far]
            put = zc
        from_rows = pl.ds(pl.multiple_of((j * ZC + take) * CHUNK, 16), CHUNK)
        to_rows = pl.ds(pl.multiple_of((j * ZC + put) * CHUNK, 16), CHUNK)
        if i == 0 and j == 0:
            return pltpu.make_async_copy(src.at[from_rows], dst.at[to_rows], recv.at[0])
        return pltpu.make_async_remote_copy(
            src_ref=src.at[from_rows],
            dst_ref=dst.at[to_rows],
            send_sem=send.at[j * ZC + i],
            recv_sem=recv.at[j * ZC + spot * 2 + flip],
            device_id=(zlt * NY + y, xt * ZC + zt * 2 + ct),
            device_id_type=MESH,
        )

    def arrival(src, dst, send, recv, j, i):
        rows = pl.ds((j * ZC + i) * CHUNK, CHUNK)
        return pltpu.make_async_remote_copy(
            src_ref=src.at[rows],
            dst_ref=dst.at[rows],
            send_sem=send.at[j * ZC + i],
            recv_sem=recv.at[j * ZC + i],
            device_id=(partner, me),
            device_id_type=MESH,
        )

    sent = []

    def start_group(src, dst, send, recv, j, sign):
        for i in range(ZC):
            copy = exchange(src, dst, send, recv, j, i, sign)
            copy.start()
            if i or j:
                sent.append(copy)

    def wait_group(src, dst, send, recv, j, sign):
        for i in range(ZC):
            if i or j:
                arrival(src, dst, send, recv, j, i).wait_recv()
            else:
                exchange(src, dst, send, recv, j, i, sign).wait()

    def pack(blocks):
        return dot(tos[...], jnp.concatenate(blocks, axis=0)).astype(BF16)

    def unpack(src, dst, j):
        rows = dot(toa[...], src[j * GROUP : (j + 1) * GROUP, :]).astype(BF16)
        for c in range(CB):
            dst[c, j * ROWS : (j + 1) * ROWS, :] = rows[c * ROWS : (c + 1) * ROWS, :]

    def gather(sel, tokens, dst, j):
        rows = dot(sel[j * ROWS : (j + 1) * ROWS, :], tokens[...]).astype(BF16)
        dst[j * GROUP : (j + 1) * GROUP, :] = pack(
            [rows[:, c * CW : (c + 1) * CW] for c in range(CB)]
        )

    def start_out(n):
        if n % 2 == 0 and n < 2 * NX:
            start_group(s_x, r_x, sx_sem, rx_sem, n // 2, 1)
        elif n < 2 * NX:
            start_group(s_s, r_s, sd_sem, rd_sem, n // 2, 1)

    for n in range(2 * NX):
        if n % 2 == 0:
            gather(pick, x_ref, s_x, n // 2)
        else:
            gather(pickp, dy_ref, s_s, n // 2)
        if n == 0:
            pl.semaphore_wait(barrier, 10 * NX - 1 + NY)
        if n < AHEAD:
            start_out(n)

    def to_y(src, dst, send, recv, k):
        return pltpu.make_async_remote_copy(
            src_ref=src,
            dst_ref=dst,
            send_sem=send,
            recv_sem=recv,
            device_id=(zl * NY + lax.rem(y + k, NY), me),
            device_id_type=MESH,
        )

    def block_of(b):
        return zl if b else 1 - zl

    def slice_copy(src, dst, send, recv, k, b, j):
        part = pl.ds(j * ROWS, ROWS)
        n = ((k - 1) * 2 + b) * NX + j
        yt = lax.rem(y + k, NY)
        return to_y(
            src.at[block_of(b) * NY + yt, part], dst.at[k, b, part], send.at[n], recv.at[n], k
        )

    def start_slices(src, dst, send, recv, j, b):
        for k in range(1, NY):
            copy = slice_copy(src, dst, send, recv, k, b, j)
            copy.start()
            sent.append(copy)

    def wait_slices(src, dst, send, recv, b):
        for j in range(NX):
            for k in range(1, NY):
                slice_copy(src, dst, send, recv, k, b, j).wait_recv()

    def piece_copy(src, dst, send, recv, k, q):
        part = pl.ds(q * ROWS, ROWS)
        n = (k - 1) * NX + q
        if k == 2:
            hop = 1 + 2 * (q % 2)
            return to_y(dst.at[hop, part], dst.at[2, part], send.at[n], recv.at[n], hop)
        return to_y(src.at[part], dst.at[k, part], send.at[n], recv.at[n], k)

    def hid_copy(k, q):
        return piece_copy(hid, dh, yh_s, yh_r, k, q)

    def gate_copy(k, q):
        cols = pl.ds(0, HW)
        return piece_copy(gu.at[:, cols], dgu.at[:, :, cols], yg_s, yg_r, k, q)

    def up_copy(k, q):
        cols = pl.ds(HW, HW)
        return piece_copy(gu.at[:, cols], dgu.at[:, :, cols], yu_s, yu_r, k, q)

    def begin(copy):
        copy.start()
        sent.append(copy)

    def pass_on(piece, q):
        piece(1 + 2 * (q % 2), q).wait_recv()
        begin(piece(2, q))

    def start_piece(piece, q):
        begin(piece(1 + 2 * (q % 2), q))
        begin(piece(3 - 2 * (q % 2), q))

    def start_back(j):
        start_group(s_b, r_b, sb_sem, rb_sem, j, -1)

    for j in range(NX):
        part = slice(j * ROWS, (j + 1) * ROWS)
        wait_group(s_x, r_x, sx_sem, rx_sem, j, 1)
        start_out(2 * j + AHEAD)
        unpack(r_x, a_x, j)
        start_slices(a_x, xs, yx_s, yx_r, j, 0)
        if j == 0:
            for load in loads:
                load.wait()
        rows = jnp.concatenate([a_x[c, part, :] for c in range(CB)], axis=1)
        for n in range(HW // CW):
            cols = slice(n * CW, (n + 1) * CW)
            gate_pre = dot(rows, wgu[:, n * CW : (n + 1) * CW])
            up_pre = dot(rows, wgu[:, HW + n * CW : HW + (n + 1) * CW])
            sig = 1.0 / (1.0 + jnp.exp(-gate_pre))
            gate_act = gate_pre * sig
            act[part, cols] = gate_act
            gfac[part, cols] = up_pre * sig * (1.0 + gate_pre * (1.0 - sig))
            hid[part, cols] = (gate_act * up_pre).astype(BF16)
        start_piece(hid_copy, j)
        if j == NX - 1:
            start_back(0)
        wait_group(s_s, r_s, sd_sem, rd_sem, j, 1)
        start_out(2 * j + 1 + AHEAD)
        if j == NX - 1:
            start_back(1)
            start_back(2)
        unpack(r_s, a_s, j)
        rows = jnp.concatenate([a_s[c, part, :] for c in range(CB)], axis=1)
        for n in range(HW // CW):
            cols = slice(n * CW, (n + 1) * CW)
            hidden_grad = dot(rows, wd[:, n * CW : (n + 1) * CW])
            gu[part, cols] = (hidden_grad * gfac[part, cols]).astype(BF16)
            gu[part, HW + n * CW : HW + (n + 1) * CW] = (hidden_grad * act[part, cols]).astype(BF16)
        start_slices(a_s, ss, ys_s, ys_r, j, 0)
        start_piece(gate_copy, j)
        deltas = gu[part, :]
        s_b[j * GROUP : (j + 1) * GROUP, :] = pack(
            [dot(deltas, wgu[c * CW : (c + 1) * CW, :], 1, 1).astype(BF16) for c in range(CB)]
        )
        if j == NX - 1:
            start_back(j)
        if j > 0:
            pass_on(hid_copy, j - 1)
            pass_on(gate_copy, j - 1)
            if j < NX - 1:
                start_piece(up_copy, j - 1)
    pass_on(hid_copy, NX - 1)

    def z_copy(n):
        return pltpu.make_async_remote_copy(
            src_ref=z_s.at[n],
            dst_ref=got_hbm.at[n],
            send_sem=zz_s.at[n],
            recv_sem=zz_r.at[n],
            device_id=(partner, me),
            device_id_type=MESH,
        )

    def sums(slices, mine, b, right):
        total = dot(mine[block_of(b) * NY + y], right(0), 0, 0)
        for k in range(1, NY):
            total = total + dot(slices[k, b], right(k), 0, 0)
        return total

    def hid_of(k):
        return hid[...] if k == 0 else dh[k]

    def gate_of(k):
        return gu[:, :HW] if k == 0 else dgu[k, :, :HW]

    def up_of(k):
        return gu[:, HW:] if k == 0 else dgu[k, :, HW:]

    def send_sums(n, slices, mine, right):
        z_s[n] = sums(slices, mine, 0, right).astype(BF16)
        begin(z_copy(n))

    def out_copy(n):
        return pltpu.make_async_copy(own.at[n], own_hbm.at[n], osem.at[n])

    def keep_sums(n, slices, mine, right):
        own[n] = sums(slices, mine, 1, right)
        out_copy(n).start()

    def wait_pieces(piece):
        for q in range(NX):
            piece(3 - 2 * (q % 2), q).wait_recv()
            piece(2, q).wait_recv()

    pass_on(gate_copy, NX - 1)
    for j in range(NX):
        if j < 2:
            start_piece(up_copy, NX - 2 + j)
        else:
            pass_on(up_copy, j - 2)
    wait_slices(a_s, ss, ys_s, ys_r, 0)
    wait_pieces(hid_copy)
    send_sums(2, ss, a_s, hid_of)
    wait_slices(a_x, xs, yx_s, yx_r, 0)
    wait_pieces(gate_copy)
    send_sums(0, xs, a_x, gate_of)
    for j in range(NX):
        if j > 1:
            pass_on(up_copy, j)
    for j in range(NX):
        start_slices(a_s, ss, ys_s, ys_r, j, 1)
        start_slices(a_x, xs, yx_s, yx_r, j, 1)
    wait_pieces(up_copy)
    send_sums(1, xs, a_x, up_of)

    for j in range(NX):
        wait_group(s_b, r_b, sb_sem, rb_sem, j, -1)
        unpack(r_b, a_b, j)
    for c in range(CB):
        xg[:, c * CW : (c + 1) * CW] = dot(pick[...], a_b[c], 0, 0).astype(BF16)
    wait_slices(a_s, ss, ys_s, ys_r, 1)
    keep_sums(2, ss, a_s, hid_of)
    wait_slices(a_x, xs, yx_s, yx_r, 1)
    keep_sums(0, xs, a_x, gate_of)
    keep_sums(1, xs, a_x, up_of)
    x_copy = pltpu.make_async_copy(xg, xg_hbm, osem.at[3])
    x_copy.start()
    for n in (2, 0, 1):
        out_copy(n).wait()
    x_copy.wait()
    for copy in sent:
        copy.wait_send()
    for n in (2, 0, 1):
        z_copy(n).wait_recv()


def finish(xg_in, own_in, got_in, xg_out, g_out, u_out, d_out, xv, own, got, isem, osem):
    loads = [
        (
            pltpu.make_async_copy(own_in.at[n], own.at[n], isem.at[n]),
            pltpu.make_async_copy(got_in.at[n], got.at[n], isem.at[3 + n]),
        )
        for n in range(3)
    ]
    x_load = pltpu.make_async_copy(xg_in, xv, isem.at[6])
    for a, b in loads:
        a.start()
        b.start()
    x_load.start()
    stores = []
    for n, out in enumerate((g_out, u_out, d_out)):
        for load in loads[n]:
            load.wait()
        own[n] += got[n].astype(F32)
        stores.append(pltpu.make_async_copy(own.at[n], out, osem.at[n]))
        stores[-1].start()
    x_load.wait()
    stores.append(pltpu.make_async_copy(xv, xg_out, osem.at[3]))
    stores[-1].start()
    for store in stores:
        store.wait()


def on_device(x_tokens, dy_tokens, probs, ids, w_gate, w_up, w_down):
    r = np.arange(GROUP)
    c, rest = r // ROWS, r % ROWS
    tgt = (rest // CAP) * CHUNK + c * CAP + rest % CAP
    inv = np.argsort(tgt)
    vmem = pl.BlockSpec(memory_space=pltpu.VMEM)
    anywhere = pl.BlockSpec(memory_space=pl.ANY)
    dma = pltpu.SemaphoreType.DMA
    grad = jax.ShapeDtypeStruct((D // 8, HW), F32)
    chunks = pltpu.VMEM((NX * GROUP, CW), BF16)
    slots = pltpu.VMEM((CB, SLOTS, CW), BF16)
    x_grad = jax.ShapeDtypeStruct((TOK, D), BF16)
    thirds = (3, D // 8, HW)
    parts = pl.pallas_call(
        kernel,
        out_shape=(
            x_grad,
            jax.ShapeDtypeStruct(thirds, F32),
            jax.ShapeDtypeStruct(thirds, BF16),
        ),
        in_specs=[vmem] * 6 + [anywhere] * 3,
        out_specs=[anywhere] * 3,
        scratch_shapes=[
            pltpu.VMEM((D, 2 * HW), BF16),
            pltpu.VMEM((D, HW), BF16),
            pltpu.VMEM((SLOTS, TOK), BF16),
            pltpu.VMEM((SLOTS, TOK), BF16),
            pltpu.VMEM((GROUP, GROUP), BF16),
            pltpu.VMEM((GROUP, GROUP), BF16),
        ]
        + [chunks] * 6
        + [slots] * 3
        + [
            pltpu.VMEM((SLOTS, HW), F32),
            pltpu.VMEM((SLOTS, HW), F32),
            pltpu.VMEM((SLOTS, HW), BF16),
            pltpu.VMEM((SLOTS, 2 * HW), BF16),
            pltpu.VMEM((NY, 2, SLOTS, CW), BF16),
            pltpu.VMEM((NY, 2, SLOTS, CW), BF16),
            pltpu.VMEM((NY, SLOTS, HW), BF16),
            pltpu.VMEM((NY, SLOTS, 2 * HW), BF16),
            pltpu.VMEM(thirds, BF16),
            pltpu.VMEM(thirds, F32),
            pltpu.VMEM((TOK, D), BF16),
            dma((3,)),
            dma((4,)),
        ]
        + [dma((NX * ZC,))] * 6
        + [dma((6 * NX,))] * 4
        + [dma((3 * NX,))] * 6
        + [dma((3,))] * 2,
        compiler_params=pltpu.CompilerParams(
            collective_id=0, has_side_effects=True, vmem_limit_bytes=60 << 20
        ),
    )(
        ids.T,
        probs.T,
        jnp.asarray(tgt, jnp.int32)[None],
        jnp.asarray(inv, jnp.int32)[None],
        x_tokens,
        dy_tokens,
        w_gate,
        w_up,
        w_down,
    )
    x_grad, gate_grad, up_grad, down_grad = pl.pallas_call(
        finish,
        out_shape=(x_grad, grad, grad, grad),
        in_specs=[anywhere] * 3,
        out_specs=[anywhere] * 4,
        scratch_shapes=[
            pltpu.VMEM((TOK, D), BF16),
            pltpu.VMEM(thirds, F32),
            pltpu.VMEM(thirds, BF16),
            dma((7,)),
            dma((4,)),
        ],
    )(*parts)
    return (x_grad, gate_grad[None], up_grad[None], down_grad[None])


def solution(mesh):
    rows = P(("dp", "expert"), None)
    held = P("expert", None, None)
    owned = P("expert", "dp", None)
    return jax.shard_map(
        on_device,
        mesh=mesh,
        in_specs=(rows, rows, rows, rows, held, held, held),
        out_specs=(rows, owned, owned, owned),
        check_vma=False,
    )
```
